32 devices in a mesh: fsdp: 32 (over z, y, x, core).
Axes of the slice: x: 2, y: 2, z: 4, core: 2. Of those that a mesh axis runs over, the one named last changes fastest.
Arguments:
- tokens: bfloat16 [2, 10240, 1024], P(None, 'fsdp'), may hold values from -6 to 6
- segment_ids: int32 [2, 10240], P(None, 'fsdp'), may hold values from -1 to 4, as said below
- cotangent: bfloat16 [2, 10240, 1024], P(None, 'fsdp'), may hold values from -6 to 6
- norm1_gain: bfloat16 [1024], P('fsdp'), may hold values from 0.25 to 1.75
- norm1_bias: bfloat16 [1024], P('fsdp'), may hold values from -3 to 3
- qkv_weight: bfloat16 [1024, 3072], P(None, 'fsdp'), may hold values from -0.1875 to 0.1875
- qv_bias: bfloat16 [2048], P('fsdp'), may hold values from -3 to 3
- proj_weight: bfloat16 [1024, 1024], P(None, 'fsdp'), may hold values from -0.875 to 0.875
- proj_bias: bfloat16 [1024], P('fsdp'), may hold values from -3 to 3
- norm2_gain: bfloat16 [1024], P('fsdp'), may hold values from 0.25 to 1.75
- norm2_bias: bfloat16 [1024], P('fsdp'), may hold values from -3 to 3
- fc1_weight: bfloat16 [1024, 4096], P(None, 'fsdp'), may hold values from -0.1875 to 0.1875
- fc1_bias: bfloat16 [4096], P('fsdp'), may hold values from -3 to 3
- fc2_weight: bfloat16 [4096, 1024], P(None, 'fsdp'), may hold values from -0.09375 to 0.09375
- fc2_bias: bfloat16 [1024], P('fsdp'), may hold values from -3 to 3
Outputs:
- activations: bfloat16 [2, 10240, 1024], P(None, 'fsdp')
- input_grad: float32 [2, 10240, 1024], P(None, 'fsdp')
- norm1_gain_grad: float32 [1024], P('fsdp')
- norm1_bias_grad: float32 [1024], P('fsdp')
- qkv_weight_grad: float32 [1024, 3072], P(None, 'fsdp')
- qv_bias_grad: float32 [2048], P('fsdp')
- proj_weight_grad: float32 [1024, 1024], P(None, 'fsdp')
- proj_bias_grad: float32 [1024], P('fsdp')
- norm2_gain_grad: float32 [1024], P('fsdp')
- norm2_bias_grad: float32 [1024], P('fsdp')
- fc1_weight_grad: float32 [1024, 4096], P(None, 'fsdp')
- fc1_bias_grad: float32 [4096], P('fsdp')
- fc2_weight_grad: float32 [4096, 1024], P(None, 'fsdp')
- fc2_bias_grad: float32 [1024], P('fsdp')
The draws below stay inside these ranges and needn't reach their ends.
Inputs may be any that keep to these rules, and one draw needn't show every extreme that they name: `segment_ids`: each aligned block of 320 rows (one device's rows of one micro-batch) holds whole images numbered 0, 1, 2 and so on in order, each of 64 to 320 rows, followed by padding rows marked -1; in each draw some image has exactly 320 rows, some block is filled by images of 64 rows, and some block ends in padding.
All inputs are finite; a program needn't handle non-finite values.
Results may differ from the reference program's by a relative error of at most 0.012.
Values may be sent and summed in bfloat16 or wider, within the bound.
No kernel may reach another device: no remote copies, remote signals or barrier semaphores. Data moves between devices by JAX's collectives and lax.ppermute only.
A program may use at most 256 MiB of HBM per device.

```python
import jax
import jax.numpy as jnp
from jax import lax

D = 1024
HDIM = 64
FF = 4096
BUFFER = 64
IMAGE = 320
ROWS = 320
MB = 2
TOKENS = 10240
N_FSDP = 32


def draw_segment_ids(key, part):
    block_count = MB * TOKENS // ROWS
    most_images = ROWS // BUFFER
    lengths = BUFFER + jax.random.randint(jax.random.fold_in(key, 11), (block_count, most_images), 0, IMAGE - BUFFER + 1)
    forced = jax.random.randint(jax.random.fold_in(key, 12), (), 0, block_count)
    filled_block = (forced + 1) % block_count
    padded_block = (forced + 2) % block_count
    lengths = lengths.at[forced, 0].set(IMAGE)
    lengths = lengths.at[filled_block].set(BUFFER)
    lengths = lengths.at[padded_block].set(BUFFER)
    lengths = lengths.at[padded_block, 0].set(BUFFER + 1)
    image_ends = jnp.cumsum(lengths, axis=1)
    position = jnp.arange(ROWS)
    number = jnp.sum((position[None, :, None] >= image_ends[:, None, :]).astype(jnp.int32), axis=2)
    last_end = jnp.max(jnp.where(image_ends <= ROWS, image_ends, 0), axis=1)
    segment_rows = jnp.where(position[None, :] < last_end[:, None], number, -1)
    return segment_rows.reshape(MB, TOKENS).astype(jnp.int32)


def strengthened(result, rng, source, target, parts, factor):
    def block_of(dim):
        return (jnp.arange(result.shape[dim]) // (result.shape[dim] // parts)).reshape((-1,) + (1,) * (result.ndim - 1 - dim))

    first = jax.random.permutation(rng, parts)[block_of(target)]
    far = (block_of(target) + parts // 2) % parts
    return jnp.where((block_of(source) == first) | (block_of(source) == far), factor * result, result)


def levels(own_key, shape, split, smallest, top_value):
    factor_of, own = 1.0, jax.random.fold_in(own_key, 6)
    for dim, shards_of in split:
        heights = jnp.exp(jax.random.uniform(jax.random.fold_in(own, dim), (shards_of,), jnp.float32, smallest / len(split), top_value / len(split)))
        factor_of = factor_of * jnp.repeat(heights, shape[dim] // shards_of).reshape([-1 if axis == dim else 1 for axis in range(len(shape))])
    return factor_of


def bell_draw(rng, dims, scale, bound, cuts=(), dtype=jnp.bfloat16):
    loudness = levels(rng, dims, cuts, -0.22, 0.18) if cuts else 1.0
    values = jax.random.normal(rng, dims, jnp.float32) * scale * loudness
    return jnp.minimum(jnp.maximum(values, -bound), bound).astype(dtype)


def noise_with(rng, extent, deviation, most, cuts, heavy, dtype=jnp.bfloat16):
    entries = deviation * jax.random.normal(rng, extent, jnp.float32)
    if cuts:
        entries = entries * levels(rng, extent, cuts, -0.22, 0.18)
    return jnp.clip(strengthened(entries, jax.random.fold_in(rng, 3), *heavy), -most, most).astype(dtype)


def setup_inputs(seed: int = 0) -> dict:
    streams_of = jax.random.split(jax.random.key(seed), 16)
    tokens = bell_draw(streams_of[0], (MB, TOKENS, D), 1.0, 6.0, ((1, 32),))
    segment_ids = draw_segment_ids(jax.random.fold_in(streams_of[15], 71), 0)
    cotangent = noise_with(streams_of[2], (MB, TOKENS, D), 1.0, 6.0, ((1, 32),), (1, 2, 32, 2.75))
    norm1_gain = jnp.clip(1.0 + 0.15 * jax.random.normal(streams_of[3], (D,), jnp.float32), 0.25, 1.75).astype(jnp.bfloat16)
    norm1_bias = bell_draw(streams_of[4], (D,), 0.5, 3.0, ((0, 32),))
    qkv_weight = bell_draw(streams_of[5], (D, 3 * D), D ** -0.5, 0.1875, ((1, 32),))
    qv_bias = bell_draw(streams_of[6], (2 * D,), 0.5, 3.0, ((0, 32),))
    proj_weight = bell_draw(streams_of[7], (D, D), (D * 16 // IMAGE) ** -0.5, 0.875, ((1, 32),))
    proj_bias = bell_draw(streams_of[8], (D,), 0.5, 3.0, ((0, 32),))
    norm2_gain = jnp.clip(1.0 + 0.15 * jax.random.normal(streams_of[9], (D,), jnp.float32), 0.25, 1.75).astype(jnp.bfloat16)
    norm2_bias = bell_draw(streams_of[10], (D,), 0.5, 3.0, ((0, 32),))
    fc1_weight = bell_draw(streams_of[11], (D, FF), D ** -0.5, 0.1875, ((1, 32),))
    fc1_bias = bell_draw(streams_of[12], (FF,), 0.5, 3.0, ((0, 32),))
    fc2_weight = bell_draw(streams_of[13], (FF, D), FF ** -0.5, 0.09375, ((1, 32),))
    fc2_bias = bell_draw(streams_of[14], (D,), 0.5, 3.0, ((0, 32),))
    return dict(tokens=tokens, segment_ids=segment_ids, cotangent=cotangent, norm1_gain=norm1_gain, norm1_bias=norm1_bias, qkv_weight=qkv_weight, qv_bias=qv_bias, proj_weight=proj_weight, proj_bias=proj_bias, norm2_gain=norm2_gain, norm2_bias=norm2_bias, fc1_weight=fc1_weight, fc1_bias=fc1_bias, fc2_weight=fc2_weight, fc2_bias=fc2_bias)


precise = lax.Precision.HIGHEST

@jax.custom_vjp
def low(v):
    return lax.optimization_barrier(v.astype(jnp.bfloat16)).astype(jnp.float32)

@jax.custom_vjp
def low_back(v):
    return v

def low_keep(v):
    return (low(v), None)

def low_pass(kept, grad):
    return (grad,)

def back_keep(v):
    return (v, None)

def back_low(kept, grad):
    return (low(grad),)
low.defvjp(low_keep, low_pass)
low_back.defvjp(back_keep, back_low)

def layer_norm(values, scale_vec, shift_vec):
    average = lax.optimization_barrier(jnp.mean(values, axis=-1, keepdims=True))
    centred = values - average
    spread = lax.optimization_barrier(jnp.mean(centred * centred, axis=-1, keepdims=True))
    return centred * lax.rsqrt(spread + 1e-06) * scale_vec + shift_vec

def block_layer(params, inputs, segment_row):
    gain_one, shift_one, qkv_w, qv_b, proj_w, proj_b, gain_two, shift_two, fc1_w, fc1_b, fc2_w, fc2_b = params
    head_count = D // HDIM
    scaling = HDIM ** (-0.5)
    valid_rows = (segment_row >= 0).astype(jnp.float32)[:, None]
    position = jnp.arange(ROWS)
    allowed = (segment_row[:, None] == segment_row[None, :]) & (segment_row[None, :] >= 0) | (position[:, None] == position[None, :])
    normed_one = low(layer_norm(inputs, gain_one, shift_one))
    projected = jnp.dot(normed_one, qkv_w, precision=precise)
    queries = low(low_back(projected[:, :D] + qv_b[:D])).reshape(ROWS, head_count, HDIM)
    key_rows = low(low_back(projected[:, D:2 * D])).reshape(ROWS, head_count, HDIM)
    values = low(low_back(projected[:, 2 * D:] + qv_b[D:])).reshape(ROWS, head_count, HDIM)
    scores = jnp.einsum('qhe,khe->hqk', queries, key_rows, precision=precise) * scaling
    scores = low_back(jnp.where(allowed[None], scores, -1e+30))
    attn_probs = jax.nn.softmax(scores, axis=-1)
    attended = jnp.einsum('hqk,khe->qhe', low(attn_probs), values, precision=precise).reshape(ROWS, D)
    attended = low(low_back(attended))
    branch = low_back(jnp.dot(attended, proj_w, precision=precise) + proj_b)
    hidden = inputs + valid_rows * branch
    normed_two = low(layer_norm(hidden, gain_two, shift_two))
    pre_act = low_back(jnp.dot(normed_two, fc1_w, precision=precise) + fc1_b)
    activated = low(jax.nn.gelu(pre_act, approximate=False))
    mlp_out = low_back(jnp.dot(activated, fc2_w, precision=precise) + fc2_b)
    return hidden + valid_rows * mlp_out

def reference(tokens, segment_ids, cotangent, norm1_gain, norm1_bias, qkv_weight, qv_bias, proj_weight, proj_bias, norm2_gain, norm2_bias, fc1_weight, fc1_bias, fc2_weight, fc2_bias):
    params = tuple((weight_arg.astype(jnp.float32) for weight_arg in (norm1_gain, norm1_bias, qkv_weight, qv_bias, proj_weight, proj_bias, norm2_gain, norm2_bias, fc1_weight, fc1_bias, fc2_weight, fc2_bias)))
    block_count = MB * N_FSDP
    block_inputs = tokens.reshape(block_count, ROWS, D).astype(jnp.float32)
    block_segs = segment_ids.reshape(block_count, ROWS)
    block_cot = cotangent.reshape(block_count, ROWS, D).astype(jnp.float32)

    def visit(running, pieces):
        inputs, segment_row, cot_rows = pieces
        output, pullback = jax.vjp(lambda weights, rows_in: block_layer(weights, rows_in, segment_row), params, inputs)
        grad_params, grad_inputs = pullback(cot_rows)
        running = jax.tree.map(jnp.add, running, grad_params)
        return (running, (output.astype(jnp.bfloat16), grad_inputs))
    zero_grads = jax.tree.map(jnp.zeros_like, params)
    totals, (outputs, grad_rows) = lax.scan(visit, zero_grads, (block_inputs, block_segs, block_cot))
    activations = outputs.reshape(MB, TOKENS, D)
    input_grad = grad_rows.reshape(MB, TOKENS, D)
    return (activations, input_grad, totals[0], totals[1], totals[2], totals[3], totals[4], totals[5], totals[6], totals[7], totals[8], totals[9], totals[10], totals[11])
```

```python
import functools

import jax
import jax.numpy as jnp
import numpy as np
from jax import lax
from jax.experimental import pallas as pl
from jax.experimental.pallas import tpu as pltpu
from jax.sharding import PartitionSpec as P

HDIM = 64
AXIS = "fsdp"
BF16 = jnp.bfloat16
F32 = jnp.float32


class Grid:
    def __init__(self, count):
        self.count = count
        chips = count // 2
        if chips == 16:
            sizes, line = (4, 2, 2), 0
        elif chips == 128:
            sizes, line = (4, 4, 8), 2
        else:
            sizes, line = (chips, 1, 1), 0
        self.sizes = sizes
        self.line = line
        self.pair = tuple(a for a in range(3) if a != line)
        self.n_line = sizes[line]
        self.n_side = sizes[self.pair[0]]
        assert sizes[self.pair[0]] == sizes[self.pair[1]]
        self.half = chips

    def coords(self, index):
        core = index % 2
        chip = index // 2
        a, b, c = self.sizes
        return [chip // (b * c), (chip // c) % b, chip % c], core

    def index(self, where, core):
        a, b, c = self.sizes
        return ((where[0] % a * b + where[1] % b) * c + where[2] % c) * 2 + core

    def axis_of(self, phase, core):
        if phase == 0:
            return self.line
        return self.pair[(phase - 1) ^ core]

    def moved(self, index, phase, shift):
        where, core = self.coords(index)
        where[self.axis_of(phase, core)] += shift
        return self.index(where, core)

    def pairs(self, phase, shift):
        return [(i, self.moved(i, phase, shift)) for i in range(self.count)]

    def swap(self):
        return [(i, i ^ 1) for i in range(self.count)]

    def slots(self, me):
        where, core = self.coords(me)
        found = []
        for q in range(self.n_side):
            for p in range(self.n_side):
                for k in range(self.n_line):
                    there = list(where)
                    there[self.axis_of(2, core)] -= q
                    there[self.axis_of(1, core)] -= p
                    there[self.line] -= k
                    found.append(self.index(there, core))
        return found

    def table(self):
        return np.array(
            [self.slots(i) + self.slots(i ^ 1) for i in range(self.count)], np.int32
        )


def _starts(copies):
    for copy in copies:
        copy.start()


def order_kernel(splits, counts, table, *refs):
    n_src = len(counts)
    sources = refs[:n_src]
    outs = refs[n_src : n_src + len(splits)]
    held, sem_in, sem_out = refs[n_src + len(splits) :]
    incoming, at = [], 0
    for k, size in enumerate(counts):
        incoming.append(
            pltpu.make_async_copy(sources[k], held.at[pl.ds(at, size)], sem_in.at[k])
        )
        at += size
    _starts(incoming)
    outgoing, at = [], 0
    for k, size in enumerate(counts):
        incoming[k].wait()
        for s in range(at, at + size):
            place = table[s]
            row = 0
            for o, rows in enumerate(splits):
                copy = pltpu.make_async_copy(
                    held.at[s, pl.ds(row, rows)], outs[o].at[place], sem_out.at[s, o]
                )
                copy.start()
                outgoing.append(copy)
                row += rows
        at += size
    for copy in outgoing:
        copy.wait()


def put_in_order(sources, table, splits):
    rows, width = sources[0].shape[-2:]
    counts = [s.shape[0] for s in sources]
    total = sum(counts)
    space = pl.BlockSpec(memory_space=pl.ANY)
    moved = 2 * 2 * total * rows * width
    return pl.pallas_call(
        functools.partial(order_kernel, tuple(splits), tuple(counts)),
        out_shape=[jax.ShapeDtypeStruct((total, r, width), BF16) for r in splits],
        grid_spec=pltpu.PrefetchScalarGridSpec(
            num_scalar_prefetch=1,
            grid=(),
            in_specs=[space] * len(sources),
            out_specs=[space] * len(splits),
            scratch_shapes=[
                pltpu.VMEM((total, rows, width), BF16),
                pltpu.SemaphoreType.DMA((len(sources),)),
                pltpu.SemaphoreType.DMA((total, len(splits))),
            ],
        ),
        cost_estimate=pl.CostEstimate(flops=0, bytes_accessed=moved, transcendentals=0),
        name="order",
    )(table, *sources)


def pack_kernel(splits, half, table, *refs):
    n_src = len(splits)
    sources = refs[:n_src]
    mine, theirs = refs[n_src : n_src + 2]
    held, sem_in, sem_out = refs[n_src + 2 :]
    incoming = []
    for s in list(range(half, 2 * half)) + list(range(half)):
        place = table[s]
        row, copies = 0, []
        for o, rows in enumerate(splits):
            copy = pltpu.make_async_copy(
                sources[o].at[place], held.at[s, pl.ds(row, rows)], sem_in.at[s, o]
            )
            copy.start()
            copies.append(copy)
            row += rows
        incoming.append((s, copies))
    for s, copies in incoming:
        for copy in copies:
            copy.wait()
        if s == 2 * half - 1:
            pltpu.make_async_copy(
                held.at[pl.ds(half, half)], theirs, sem_out.at[1]
            ).start()
        if s == half - 1:
            pltpu.make_async_copy(held.at[pl.ds(0, half)], mine, sem_out.at[0]).start()
    pltpu.make_async_copy(held.at[pl.ds(half, half)], theirs, sem_out.at[1]).wait()
    pltpu.make_async_copy(held.at[pl.ds(0, half)], mine, sem_out.at[0]).wait()


def pack(sources, table, half):
    splits = [s.shape[1] for s in sources]
    rows, width = sum(splits), sources[0].shape[2]
    space = pl.BlockSpec(memory_space=pl.ANY)
    moved = 2 * 2 * 2 * half * rows * width
    return pl.pallas_call(
        functools.partial(pack_kernel, tuple(splits), half),
        out_shape=[jax.ShapeDtypeStruct((half, rows, width), BF16)] * 2,
        grid_spec=pltpu.PrefetchScalarGridSpec(
            num_scalar_prefetch=1,
            grid=(),
            in_specs=[space] * len(sources),
            out_specs=[space] * 2,
            scratch_shapes=[
                pltpu.VMEM((2 * half, rows, width), BF16),
                pltpu.SemaphoreType.DMA((2 * half, len(splits))),
                pltpu.SemaphoreType.DMA((2,)),
            ],
        ),
        cost_estimate=pl.CostEstimate(flops=0, bytes_accessed=moved, transcendentals=0),
        name="pack",
    )(table, *sources)


def send(value, pairs):
    return lax.ppermute(value, AXIS, pairs)


def gather_line(grid, shard):
    got = [shard] + [send(shard, grid.pairs(0, k)) for k in range(1, grid.n_line)]
    return jnp.stack(got)


def gather_sides(grid, block):
    n = grid.n_side
    near = [block] + [send(block, grid.pairs(1, k)) for k in range(1, n)]
    near = jnp.concatenate(near) if n > 1 else block
    far = [send(near, grid.pairs(2, k)) for k in range(1, n)]
    parts = [near] + far
    return parts + [send(part, grid.swap()) for part in parts]


def scatter_sum(grid, mine, theirs):
    n, line = grid.n_side, grid.n_line
    arrived = send(theirs, grid.swap())
    shape = (n, n, line) + mine.shape[1:]
    terms = [mine.reshape(shape), arrived.reshape(shape)]
    for phase in (2, 1, 0):
        size = terms[0].shape[0]
        got = []
        for k in range(1, size):
            part = sum(t[k].astype(F32) for t in terms).astype(BF16)
            got.append(send(part, grid.pairs(phase, -k)))
        terms = [t[0] for t in terms] + got
    return sum(t.astype(F32) for t in terms)


def centre(values):
    average = jnp.mean(values, axis=-1, keepdims=True)
    centred = values - average
    spread = jnp.mean(centred * centred, axis=-1, keepdims=True)
    inverse = lax.rsqrt(spread + 1e-06)
    return centred * inverse, inverse


def norm_back(grad, normal, inverse, gain):
    scaled = grad * gain
    first = jnp.mean(scaled, axis=-1, keepdims=True)
    second = jnp.mean(scaled * normal, axis=-1, keepdims=True)
    return inverse * (scaled - first - normal * second)


def nt(a, b):
    return lax.dot_general(a, b, (((1,), (1,)), ((), ())), preferred_element_type=F32)


def nn(a, b):
    return lax.dot_general(a, b, (((1,), (0,)), ((), ())), preferred_element_type=F32)


def tn(a, b):
    return lax.dot_general(a, b, (((0,), (0,)), ((), ())), preferred_element_type=F32)


def padded(rows):
    return -(-rows // 16) * 16


def pad_rows(value, rows):
    return jnp.pad(value, ((0, 0),) * (value.ndim - 2) + ((0, rows - value.shape[-2]), (0, 0)))


def body(
    grid,
    tokens,
    segment_ids,
    cotangent,
    norm1_gain,
    norm1_bias,
    qkv_weight,
    qv_bias,
    proj_weight,
    proj_bias,
    norm2_gain,
    norm2_bias,
    fc1_weight,
    fc1_bias,
    fc2_weight,
    fc2_bias,
):
    micro, rows, width = tokens.shape
    n = grid.count
    heads = width // HDIM
    all_rows = micro * rows
    table = lax.dynamic_index_in_dim(
        jnp.asarray(grid.table()), lax.axis_index(AXIS), 0, keepdims=False
    )

    smalls = (
        norm1_gain,
        norm1_bias,
        qv_bias,
        proj_bias,
        norm2_gain,
        norm2_bias,
        fc1_bias,
        fc2_bias,
    )
    small_sizes = [v.shape[0] for v in smalls]
    small = jnp.concatenate(smalls)
    small = jnp.pad(small, (0, width - small.shape[0])).reshape(1, width)
    r_qkv, r_proj = qkv_weight.shape[1], proj_weight.shape[1]
    splits = [padded(r_qkv), padded(r_proj), 8]
    shard_one = jnp.concatenate(
        [
            pad_rows(qkv_weight.T, splits[0]),
            pad_rows(proj_weight.T, splits[1]),
            pad_rows(small, splits[2]),
        ]
    )
    shard_fc1 = fc1_weight.T
    shard_fc2 = fc2_weight.T

    line_one = gather_line(grid, shard_one)
    shard_fc1, line_one = lax.optimization_barrier((shard_fc1, line_one))
    line_fc1 = gather_line(grid, shard_fc1)
    parts_one = gather_sides(grid, line_one)
    shard_fc2, line_fc1 = lax.optimization_barrier((shard_fc2, line_fc1))
    line_fc2 = gather_line(grid, shard_fc2)
    parts_fc1 = gather_sides(grid, line_fc1)
    parts_fc2 = gather_sides(grid, line_fc2)

    qkv_all, proj_all, small_all = put_in_order(parts_one, table, splits)
    qkv_t = qkv_all[:, :r_qkv].reshape(n * r_qkv, width)
    proj_t = proj_all[:, :r_proj].reshape(n * r_proj, width)
    (fc1_all,) = put_in_order(parts_fc1, table, [shard_fc1.shape[0]])
    fc1_t = fc1_all.reshape(-1, width)
    (fc2_all,) = put_in_order(parts_fc2, table, [shard_fc2.shape[0]])
    fc2_t = fc2_all.reshape(width, -1)

    vectors, at = [], 0
    small_flat = small_all[:, 0, :].astype(F32)
    for size in small_sizes:
        vectors.append(small_flat[:, at : at + size].reshape(-1))
        at += size
    gain_one, shift_one, qv_b, proj_b, gain_two, shift_two, fc1_b, fc2_b = vectors

    x = tokens.reshape(all_rows, width).astype(F32)
    valid = (segment_ids.reshape(all_rows, 1) >= 0).astype(F32)
    row_index = lax.broadcasted_iota(jnp.int32, (rows, rows), 0)
    col_index = lax.broadcasted_iota(jnp.int32, (rows, rows), 1)
    allowed = (segment_ids[:, :, None] == segment_ids[:, None, :]) & (
        segment_ids[:, None, :] >= 0
    ) | (row_index == col_index)[None]

    z_one, inv_one = centre(x)
    normed_one = (z_one * gain_one + shift_one).astype(BF16)
    projected = nt(normed_one, qkv_t)

    def split_heads(value):
        return value.astype(BF16).reshape(micro, rows, heads, HDIM)

    queries = split_heads(projected[:, :width] + qv_b[:width])
    keys = split_heads(projected[:, width : 2 * width])
    values = split_heads(projected[:, 2 * width :] + qv_b[width:])
    scaling = HDIM**-0.5

    def scores_of():
        scores = jnp.einsum("bqhe,bkhe->bhqk", queries, keys, preferred_element_type=F32)
        return jnp.where(allowed[:, None], scores * scaling, -1e30)

    scores = scores_of()
    log_total = jax.nn.logsumexp(scores, axis=-1)
    probs = jnp.exp(scores - log_total[..., None])
    attended = jnp.einsum(
        "bhqk,bkhe->bqhe", probs.astype(BF16), values, preferred_element_type=F32
    )
    attended = attended.reshape(all_rows, width).astype(BF16)
    hidden = x + valid * (nt(attended, proj_t) + proj_b)
    z_two, inv_two = centre(hidden)
    normed_two = (z_two * gain_two + shift_two).astype(BF16)
    pre_act = nt(normed_two, fc1_t) + fc1_b
    activated = jax.nn.gelu(pre_act, approximate=False).astype(BF16)
    output = hidden + valid * (nt(activated, fc2_t) + fc2_b)

    grad_out = cotangent.reshape(all_rows, width).astype(F32)
    grad_mlp = (valid * grad_out).astype(BF16)

    def reduce_group(*grads):
        return scatter_sum(grid, *pack(grads, table, grid.half))

    g_fc2 = tn(grad_mlp, activated).astype(BF16).reshape(n, -1, activated.shape[1])
    share_fc2 = reduce_group(g_fc2)
    grad_fc2_b = jnp.sum(grad_mlp.astype(F32), axis=0)
    grad_act = nn(grad_mlp, fc2_t)
    _, slope_pull = jax.vjp(lambda v: jax.nn.gelu(v, approximate=False), pre_act)
    grad_pre = slope_pull(grad_act)[0].astype(BF16)
    g_fc1 = tn(grad_pre, normed_two).astype(BF16).reshape(n, -1, width)
    share_fc1 = reduce_group(g_fc1)
    grad_fc1_b = jnp.sum(grad_pre.astype(F32), axis=0)
    grad_norm_two = nn(grad_pre, fc1_t)
    grad_gain_two = jnp.sum(grad_norm_two * z_two, axis=0)
    grad_shift_two = jnp.sum(grad_norm_two, axis=0)
    grad_hidden = grad_out + norm_back(grad_norm_two, z_two, inv_two, gain_two)
    grad_branch = (valid * grad_hidden).astype(BF16)
    g_proj = tn(grad_branch, attended).astype(BF16).reshape(n, r_proj, width)
    grad_proj_b = jnp.sum(grad_branch.astype(F32), axis=0)
    grad_att = nn(grad_branch, proj_t).astype(BF16).reshape(micro, rows, heads, HDIM)

    scores = scores_of()
    probs = jnp.exp(scores - log_total[..., None])
    grad_probs = jnp.einsum("bqhe,bkhe->bhqk", grad_att, values, preferred_element_type=F32)
    grad_values = jnp.einsum(
        "bhqk,bqhe->bkhe", probs.astype(BF16), grad_att, preferred_element_type=F32
    )
    inner = jnp.sum(probs * grad_probs, axis=-1, keepdims=True)
    grad_scores = (probs * (grad_probs - inner)).astype(BF16)
    grad_queries = scaling * jnp.einsum(
        "bhqk,bkhe->bqhe", grad_scores, keys, preferred_element_type=F32
    )
    grad_keys = scaling * jnp.einsum(
        "bhqk,bqhe->bkhe", grad_scores, queries, preferred_element_type=F32
    )
    grad_qkv = jnp.concatenate(
        [
            g.reshape(all_rows, width).astype(BF16)
            for g in (grad_queries, grad_keys, grad_values)
        ],
        axis=1,
    )
    g_qkv = tn(grad_qkv, normed_one).astype(BF16).reshape(n, r_qkv, width)
    sums = jnp.sum(grad_qkv.astype(F32), axis=0)
    grad_qv_b = jnp.concatenate([sums[:width], sums[2 * width :]])
    grad_norm_one = nn(grad_qkv, qkv_t)
    grad_gain_one = jnp.sum(grad_norm_one * z_one, axis=0)
    grad_shift_one = jnp.sum(grad_norm_one, axis=0)
    input_grad = grad_hidden + norm_back(grad_norm_one, z_one, inv_one, gain_one)

    small_grads = (
        grad_gain_one,
        grad_shift_one,
        grad_qv_b,
        grad_proj_b,
        grad_gain_two,
        grad_shift_two,
        grad_fc1_b,
        grad_fc2_b,
    )
    g_small = jnp.concatenate([g.reshape(n, -1) for g in small_grads], axis=1)
    g_small = jnp.pad(g_small, ((0, 0), (0, width - g_small.shape[1])))
    g_small = pad_rows(g_small.astype(BF16)[:, None, :], splits[2])
    share_one = reduce_group(
        pad_rows(g_qkv, splits[0]), pad_rows(g_proj, splits[1]), g_small
    )
    share_qkv = share_one[:r_qkv].T
    share_proj = share_one[splits[0] : splits[0] + r_proj].T
    row, shares, at = share_one[splits[0] + splits[1]], [], 0
    for size in small_sizes:
        shares.append(row[at : at + size])
        at += size
    s_gain_one, s_shift_one, s_qv, s_proj, s_gain_two, s_shift_two, s_fc1, s_fc2 = shares
    return (
        output.astype(BF16).reshape(micro, rows, width),
        input_grad.reshape(micro, rows, width),
        s_gain_one,
        s_shift_one,
        share_qkv,
        s_qv,
        share_proj,
        s_proj,
        s_gain_two,
        s_shift_two,
        share_fc1.T,
        s_fc1,
        share_fc2.T,
        s_fc2,
    )


def solution(mesh):
    row = P(None, AXIS, None)
    vec = P(AXIS)
    mat = P(None, AXIS)
    return jax.shard_map(
        functools.partial(body, Grid(mesh.size)),
        mesh=mesh,
        in_specs=(row, mat, row) + (vec, vec, mat, vec, mat, vec) + (vec, vec, mat, vec, mat, vec),
        out_specs=(row, row) + (vec, vec, mat, vec, mat, vec) + (vec, vec, mat, vec, mat, vec),
        check_vma=False,
    )
```

```python
import functools

import jax
import jax.numpy as jnp
import numpy as np
from jax import lax
from jax.experimental import pallas as pl
from jax.experimental.pallas import tpu as pltpu
from jax.sharding import PartitionSpec as P


HDIM = 64
AXIS = "fsdp"
BF16 = jnp.bfloat16
F32 = jnp.float32


class Grid:
    def __init__(self, count):
        self.count = count
        chips = count // 2
        if chips == 16:
            sizes, line = (4, 2, 2), 0
        elif chips == 128:
            sizes, line = (4, 4, 8), 2
        else:
            sizes, line = (chips, 1, 1), 0
        self.sizes = sizes
        self.line = line
        self.pair = tuple(a for a in range(3) if a != line)
        self.n_line = sizes[line]
        self.n_side = sizes[self.pair[0]]
        assert sizes[self.pair[0]] == sizes[self.pair[1]]
        self.half = chips

    def coords(self, index):
        core = index % 2
        chip = index // 2
        _, b, c = self.sizes
        return [chip // (b * c), (chip // c) % b, chip % c], core

    def index(self, where, core):
        a, b, c = self.sizes
        return ((where[0] % a * b + where[1] % b) * c + where[2] % c) * 2 + core

    def axis_of(self, phase, core):
        if phase == 0:
            return self.line
        return self.pair[(phase - 1) ^ core]

    def moved(self, index, phase, shift):
        where, core = self.coords(index)
        where[self.axis_of(phase, core)] += shift
        return self.index(where, core)

    def pairs(self, phase, shift):
        return [(i, self.moved(i, phase, shift)) for i in range(self.count)]

    def swap(self):
        return [(i, i ^ 1) for i in range(self.count)]

    def slots(self, me):
        where, core = self.coords(me)
        found = []
        for q in range(self.n_side):
            for p in range(self.n_side):
                for k in range(self.n_line):
                    there = list(where)
                    there[self.axis_of(2, core)] -= q
                    there[self.axis_of(1, core)] -= p
                    there[self.line] -= k
                    found.append(self.index(there, core))
        return found

    def table(self):
        return np.array(
            [self.slots(i) + self.slots(i ^ 1) for i in range(self.count)], np.int32
        )


    def where(self):
        table = self.table()
        found = np.zeros((self.count, self.count + 1), np.int32)
        for i in range(self.count):
            found[i, table[i]] = np.arange(self.count) % self.half
            found[i, -1] = i % 2
        return found


def _starts(copies):
    for copy in copies:
        copy.start()


def order_kernel(splits, counts, table, *refs):
    n_src = len(counts)
    sources = refs[:n_src]
    outs = refs[n_src : n_src + len(splits)]
    held, sem_in, sem_out = refs[n_src + len(splits) :]
    incoming, at = [], 0
    for k, size in enumerate(counts):
        incoming.append(
            pltpu.make_async_copy(sources[k], held.at[pl.ds(at, size)], sem_in.at[k])
        )
        at += size
    _starts(incoming)
    outgoing, at = [], 0
    for k, size in enumerate(counts):
        incoming[k].wait()
        for s in range(at, at + size):
            place = table[s]
            row = 0
            for o, rows in enumerate(splits):
                copy = pltpu.make_async_copy(
                    held.at[s, pl.ds(row, rows)], outs[o].at[place], sem_out.at[s, o]
                )
                copy.start()
                outgoing.append(copy)
                row += rows
        at += size
    for copy in outgoing:
        copy.wait()


def put_in_order(sources, table, splits):
    rows, width = sources[0].shape[-2:]
    counts = [s.shape[0] for s in sources]
    total = sum(counts)
    space = pl.BlockSpec(memory_space=pl.ANY)
    moved = 2 * 2 * total * rows * width
    return pl.pallas_call(
        functools.partial(order_kernel, tuple(splits), tuple(counts)),
        out_shape=[jax.ShapeDtypeStruct((total, r, width), BF16) for r in splits],
        grid_spec=pltpu.PrefetchScalarGridSpec(
            num_scalar_prefetch=1,
            grid=(),
            in_specs=[space] * len(sources),
            out_specs=[space] * len(splits),
            scratch_shapes=[
                pltpu.VMEM((total, rows, width), BF16),
                pltpu.SemaphoreType.DMA((len(sources),)),
                pltpu.SemaphoreType.DMA((total, len(splits))),
            ],
        ),
        cost_estimate=pl.CostEstimate(flops=0, bytes_accessed=moved, transcendentals=0),
    )(table, *sources)


def pack_kernel(splits, half, table, *refs):
    n_src = len(splits)
    sources = refs[:n_src]
    mine, theirs = refs[n_src : n_src + 2]
    held, sem_in, sem_out = refs[n_src + 2 :]
    incoming = []
    for s in list(range(half, 2 * half)) + list(range(half)):
        place = table[s]
        row, copies = 0, []
        for o, rows in enumerate(splits):
            copy = pltpu.make_async_copy(
                sources[o].at[place], held.at[s, pl.ds(row, rows)], sem_in.at[s, o]
            )
            copy.start()
            copies.append(copy)
            row += rows
        incoming.append((s, copies))
    for s, copies in incoming:
        for copy in copies:
            copy.wait()
        if s == 2 * half - 1:
            pltpu.make_async_copy(
                held.at[pl.ds(half, half)], theirs, sem_out.at[1]
            ).start()
        if s == half - 1:
            pltpu.make_async_copy(held.at[pl.ds(0, half)], mine, sem_out.at[0]).start()
    pltpu.make_async_copy(held.at[pl.ds(half, half)], theirs, sem_out.at[1]).wait()
    pltpu.make_async_copy(held.at[pl.ds(0, half)], mine, sem_out.at[0]).wait()


def pack(sources, table, half):
    splits = [s.shape[1] for s in sources]
    rows, width = sum(splits), sources[0].shape[2]
    space = pl.BlockSpec(memory_space=pl.ANY)
    moved = 2 * 2 * 2 * half * rows * width
    return pl.pallas_call(
        functools.partial(pack_kernel, tuple(splits), half),
        out_shape=[jax.ShapeDtypeStruct((half, rows, width), BF16)] * 2,
        grid_spec=pltpu.PrefetchScalarGridSpec(
            num_scalar_prefetch=1,
            grid=(),
            in_specs=[space] * len(sources),
            out_specs=[space] * 2,
            scratch_shapes=[
                pltpu.VMEM((2 * half, rows, width), BF16),
                pltpu.SemaphoreType.DMA((2 * half, len(splits))),
                pltpu.SemaphoreType.DMA((2,)),
            ],
        ),
        cost_estimate=pl.CostEstimate(flops=0, bytes_accessed=moved, transcendentals=0),
    )(table, *sources)


def join_kernel(count, *refs):
    sources, out, held, sem_in, sem_out = refs[:count], *refs[count:]
    copies = []
    for k, source in enumerate(sources):
        copies.append(pltpu.make_async_copy(source, held.at[k], sem_in.at[k]))
    _starts(copies)
    leaving = []
    for k, copy in enumerate(copies):
        copy.wait()
        leaving.append(pltpu.make_async_copy(held.at[k], out.at[k], sem_out.at[k]))
        leaving[-1].start()
    for copy in leaving:
        copy.wait()


def join(pieces):
    count, shape = len(pieces), pieces[0].shape
    size = int(np.prod(shape))
    space = pl.BlockSpec(memory_space=pl.ANY)
    return pl.pallas_call(
        functools.partial(join_kernel, count),
        out_shape=jax.ShapeDtypeStruct((count, *shape), BF16),
        in_specs=[space] * count,
        out_specs=space,
        scratch_shapes=[
            pltpu.VMEM((count, *shape), BF16),
            pltpu.SemaphoreType.DMA((count,)),
            pltpu.SemaphoreType.DMA((count,)),
        ],
        cost_estimate=pl.CostEstimate(
            flops=0, bytes_accessed=4 * count * size, transcendentals=0
        ),
    )(*pieces)


def first_shard_kernel(w_ref, *refs):
    smalls, out_ref = refs[:-1], refs[-1]
    rows = w_ref.shape[0]
    out_ref[:rows] = w_ref[...]
    out_ref[rows:] = jnp.zeros((out_ref.shape[0] - rows, out_ref.shape[1]), BF16)
    at = 0
    for small in smalls:
        size = small.shape[1]
        out_ref[rows : rows + 1, at : at + size] = small[...]
        at += size


def first_shard(w, smalls):
    rows, width = w.shape
    return pl.pallas_call(
        first_shard_kernel,
        out_shape=jax.ShapeDtypeStruct((rows + 8, width), BF16),
        name="first_shard",
    )(w, *[v.reshape(1, -1) for v in smalls])


def send(value, pairs):
    return lax.ppermute(value, AXIS, pairs)


def gather_line(grid, shard):
    got = [shard]
    for k in range(1, grid.n_line):
        got.append(send(shard, grid.pairs(0, k)))
    return join(got)


def gather_sides(grid, block):
    n = grid.n_side
    near = [block]
    for k in range(1, n):
        near.append(send(block, grid.pairs(1, k)))
    near = join(near).reshape(-1, *block.shape[1:])
    far = [send(near, grid.pairs(2, k)) for k in range(1, n)]
    back = [send(near, grid.swap())]
    for k, part in enumerate(far, 1):
        back.append(send(part, grid.swap()))
    return [near] + far + back


def scatter_sum(grid, mine, theirs):
    n, line = grid.n_side, grid.n_line
    arrived = send(theirs, grid.swap())
    shape = (n, n, line) + mine.shape[1:]
    terms = [mine.reshape(shape), arrived.reshape(shape)]
    for phase in (2, 1, 0):
        size = terms[0].shape[0]
        got = []
        for k in range(1, size):
            part = sum(t[k].astype(F32) for t in terms).astype(BF16)
            got.append(send(part, grid.pairs(phase, -k)))
        terms = [t[0] for t in terms] + got
    return sum(t.astype(F32) for t in terms)


def sum_everywhere(grid, value):
    value += send(value, grid.swap())
    for phase in (2, 1, 0):
        size = grid.n_line if phase == 0 else grid.n_side
        value += sum(send(value, grid.pairs(phase, k)) for k in range(1, size))
    return value


def nt(a, b):
    return lax.dot_general(a, b, (((1,), (1,)), ((), ())), preferred_element_type=F32)


def nn(a, b):
    return lax.dot_general(a, b, (((1,), (0,)), ((), ())), preferred_element_type=F32)


def tn(a, b):
    return lax.dot_general(a, b, (((0,), (0,)), ((), ())), preferred_element_type=F32)


def centre(values):
    average = jnp.mean(values, axis=-1, keepdims=True)
    centred = values - average
    spread = jnp.mean(centred * centred, axis=-1, keepdims=True)
    inverse = lax.rsqrt(spread + 1e-06)
    return centred * inverse, inverse


def norm_back(grad, normal, inverse, gain):
    scaled = grad * gain
    first = jnp.mean(scaled, axis=-1, keepdims=True)
    second = jnp.mean(scaled * normal, axis=-1, keepdims=True)
    return inverse * (scaled - first - normal * second)


def column_sum(values):
    return jnp.sum(values, axis=0, keepdims=True)


def whole(*shape):
    return pl.BlockSpec(shape, lambda *_: (0,) * len(shape))


def cols(rows, width):
    return pl.BlockSpec((rows, width), lambda i: (0, i))


def tall(rows, width):
    return pl.BlockSpec((rows, width), lambda i: (i, 0))


def call(kernel, grid, ins, outs, args, flops, scratch=(), tables=(), aliases=None):
    shapes = [jax.ShapeDtypeStruct(s, d) for s, d, _ in outs]
    size = sum(np.prod(a.shape) * a.dtype.itemsize for a in list(args) + shapes)
    return pl.pallas_call(
        kernel,
        out_shape=shapes,
        grid_spec=pltpu.PrefetchScalarGridSpec(
            num_scalar_prefetch=len(tables),
            grid=grid,
            in_specs=ins,
            out_specs=[o[2] for o in outs],
            scratch_shapes=list(scratch),
        ),
        input_output_aliases=aliases or {},
        cost_estimate=pl.CostEstimate(
            flops=int(flops), bytes_accessed=int(size), transcendentals=0
        ),
    )(*tables, *args)


def fetches(table, sources, row, rows, held, sems):
    copies, at = [], 0
    for source in sources:
        for s in range(source.shape[0]):
            copies.append(
                pltpu.make_async_copy(
                    source.at[s, pl.ds(row, rows)], held.at[table[at]], sems.at[at]
                )
            )
            at += 1
    return copies


def _waits(copies):
    for copy in copies:
        copy.wait()


def step_rows(held_ref, step, size):
    rows, width = held_ref.shape[1:]
    count = size // rows
    return held_ref[pl.ds(step * count, count)].reshape(size, width)


def share_out(place, row, rows, where_ref, held_ref, sems, mine, theirs, core):
    for j in range(held_ref.shape[0] // rows):
        slot = where_ref[place + j]
        source = held_ref.at[pl.ds(j * rows, rows)]
        for out, own in ((mine, True), (theirs, False)):

            @pl.when((core == j % 2) == own)
            def _():
                pltpu.make_async_copy(
                    source, out.at[slot, pl.ds(row, rows)], sems.at[j]
                ).start()


def shared_out(row, rows, held_ref, sems, mine):
    for j in range(held_ref.shape[0] // rows):
        source = held_ref.at[pl.ds(j * rows, rows)]
        pltpu.make_async_copy(source, mine.at[0, pl.ds(row, rows)], sems.at[j]).wait()


def shares(result, row, rows, where_ref, held_ref, sems, mine, theirs):
    step, last = pl.program_id(0), pl.num_programs(0) - 1
    now = step % 2
    count = held_ref.shape[1] // rows
    core = where_ref[where_ref.shape[0] - 1]

    @pl.when(step >= 2)
    def _():
        shared_out(row, rows, held_ref.at[now], sems.at[now], mine)

    held_ref[now] = result.astype(BF16)
    share_out(
        step * count, row, rows, where_ref, held_ref.at[now], sems.at[now],
        mine, theirs, core,
    )

    @pl.when(step == last)
    def _():
        shared_out(row, rows, held_ref.at[now], sems.at[now], mine)
        if pl.num_programs(0) > 1:
            shared_out(row, rows, held_ref.at[1 - now], sems.at[1 - now], mine)


ANY = pl.BlockSpec(memory_space=pl.ANY)
PLACES = 32


STEP = 512


GAIN_ONE, SHIFT_ONE, QV, PROJ, GAIN_TWO, SHIFT_TWO, FC2, VECTORS = 0, 1, 2, 4, 5, 6, 11, 16


def spread(piece, width):
    devices, size = piece.shape
    lane = lax.broadcasted_iota(jnp.int32, (size, width), 1)
    entry = lax.broadcasted_iota(jnp.int32, (size, width), 0)
    copied = nn(piece, (lane % size == entry).astype(BF16))
    device = lax.broadcasted_iota(jnp.int32, (devices, width), 0)
    owner = lax.broadcasted_iota(jnp.int32, (devices, width), 1) // size
    per_row = width // size
    return [
        column_sum(jnp.where(device - row * per_row == owner, copied, 0.0))
        for row in range(-(-devices * size // width))
    ]


def qkv_kernel(n_src, sizes, table, small_table, x_ref, *refs):
    sources, smalls = refs[:n_src], refs[n_src : -10]
    normed_ref, out_ref, vector_ref, fc1_ref, w_out = refs[-10:-5]
    held, small_held, bias_ref, sems, small_sems = refs[-5:]
    step = pl.program_id(0)
    _, width = x_ref.shape
    rows = held.shape[1]
    leaving = pltpu.make_async_copy(held, w_out, small_sems.at[small_held.shape[0]])

    @pl.when(step == 0)
    def _():
        small_copies = fetches(small_table, smalls, smalls[0].shape[1] - 8, 8, small_held, small_sems)
        copies = fetches(table, sources, 0, rows, held, sems)
        _starts(small_copies)
        _starts(copies)
        normal, _ = centre(x_ref[...].astype(F32))
        _waits(small_copies)
        values = small_held[:, 0, :]
        at, row = 0, 0
        vector_ref[...] = jnp.zeros(vector_ref.shape, F32)
        for number, size in enumerate(sizes):
            for k, line in enumerate(spread(values[:, at : at + size], width)):
                vector_ref[row : row + 1] = line
                if number == 6:
                    fc1_ref[:, k * width : (k + 1) * width] = line
                row += 1
            at += size
        bias_ref[:, :width] = vector_ref[QV : QV + 1]
        bias_ref[:, width : 2 * width] = jnp.zeros((1, width), F32)
        bias_ref[:, 2 * width :] = vector_ref[QV + 1 : QV + 2]
        gain, shift = vector_ref[GAIN_ONE : GAIN_ONE + 1], vector_ref[SHIFT_ONE : SHIFT_ONE + 1]
        normed_ref[...] = (normal * gain + shift).astype(BF16)
        _waits(copies)
        leaving.start()

    size = out_ref.shape[1]
    bias = bias_ref[:, pl.ds(pl.multiple_of(step * size, size), size)]
    out_ref[...] = (nt(normed_ref[...], step_rows(held, step, size)) + bias).astype(BF16)

    @pl.when(step == pl.num_programs(0) - 1)
    def _():
        leaving.wait()


def qkv_forward(x, sources, table, smalls, small_table, sizes):
    m, d = x.shape
    n = 3 * d
    rows = n // PLACES
    step = 8 * rows
    devices = sum(s.shape[0] for s in smalls)
    ff = sizes[6] * devices
    return call(
        functools.partial(qkv_kernel, len(sources), tuple(sizes)),
        (n // step,),
        [whole(m, d)] + [ANY] * (len(sources) + len(smalls)),
        [
            ((m, d), BF16, whole(m, d)),
            ((m, n), BF16, pl.BlockSpec((m, step), lambda i, *_: (0, i))),
            ((VECTORS, d), F32, whole(VECTORS, d)),
            ((1, ff), F32, whole(1, ff)),
            ((PLACES, rows, d), BF16, ANY),
        ],
        (x, *sources, *smalls),
        2 * m * d * n,
        [
            pltpu.VMEM((PLACES, rows, d), BF16),
            pltpu.VMEM((devices, 8, d), BF16),
            pltpu.VMEM((1, n), F32),
            pltpu.SemaphoreType.DMA((PLACES,)),
            pltpu.SemaphoreType.DMA((devices + 1,)),
        ],
        (table, small_table),
    )


def fill_bias(bias_ref, seg_col_ref, seg_row_ref):
    seg_q, seg_k = seg_col_ref[...], seg_row_ref[0]
    rows = seg_q.shape[0]
    row = lax.broadcasted_iota(jnp.int32, (rows, rows), 0)
    col = lax.broadcasted_iota(jnp.int32, (rows, rows), 1)
    allowed = ((seg_q == seg_k) & (seg_k >= 0)) | (row == col)
    bias_ref[...] = jnp.where(allowed, 0.0, -1e30)


def lower_lanes(shape):
    return lax.broadcasted_iota(jnp.int32, shape, 1) < HDIM


def attend_kernel(seg_col_ref, seg_row_ref, q_ref, k_ref, v_ref, out_ref, total_ref, bias_ref):
    @pl.when(pl.program_id(1) == 0)
    def _():
        fill_bias(bias_ref, seg_col_ref, seg_row_ref)

    k, v = k_ref[...], v_ref[...]
    q = q_ref[...] * (HDIM**-0.5)
    low = lower_lanes(q.shape)
    bias = bias_ref[...]
    found, totals = [], []
    for keep in (low, ~low):
        scores = nt(jnp.where(keep, q, 0), k) + bias
        most = jnp.max(scores, axis=-1, keepdims=True)
        grown = jnp.exp(scores - most)
        total = jnp.sum(grown, axis=-1, keepdims=True)
        probs = (grown * (1.0 / total)).astype(BF16)
        found.append(nn(probs, v))
        totals.append(most + jnp.log(total))
    out_ref[...] = jnp.where(low, found[0], found[1]).astype(BF16)
    total_ref[...] = jnp.where(low, totals[0], totals[1])


def head_block(rows, offset):
    return pl.BlockSpec((rows, 2 * HDIM), lambda b, h: (b, offset + h))


def attend(seg_col, seg_row, qkv, rows):
    m, d = qkv.shape[0], qkv.shape[1] // 3
    pairs = d // (2 * HDIM)
    return call(
        attend_kernel,
        (m // rows, pairs),
        [
            pl.BlockSpec((rows, 1), lambda b, h: (b, 0)),
            pl.BlockSpec((1, 1, rows), lambda b, h: (b, 0, 0)),
            head_block(rows, 0),
            head_block(rows, pairs),
            head_block(rows, 2 * pairs),
        ],
        [((m, d), BF16, head_block(rows, 0)), ((m, d), F32, head_block(rows, 0))],
        (seg_col, seg_row, qkv, qkv, qkv),
        4 * m * rows * d * 2,
        [pltpu.VMEM((rows, rows), F32)],
    )


def proj_kernel(row, table, att_ref, x_ref, valid_ref, vector_ref, *refs):
    sources = refs[:-6]
    hidden_ref, normed_ref, w_out, held, sems, leave = refs[-6:]
    rows, width = held.shape[1:]
    leaving = pltpu.make_async_copy(held, w_out, leave)

    @pl.when(pl.program_id(0) == 0)
    def _():
        copies = fetches(table, sources, row, rows, held, sems)
        _starts(copies)
        _waits(copies)
        leaving.start()

    bias = vector_ref[PROJ : PROJ + 1]
    gain, shift = vector_ref[GAIN_TWO : GAIN_TWO + 1], vector_ref[SHIFT_TWO : SHIFT_TWO + 1]
    branch = nt(att_ref[...], step_rows(held, 0, width)) + bias
    hidden = x_ref[...].astype(F32) + valid_ref[...] * branch
    hidden_ref[...] = hidden
    normal, _ = centre(hidden)
    normed_ref[...] = (normal * gain + shift).astype(BF16)

    @pl.when(pl.program_id(0) == pl.num_programs(0) - 1)
    def _():
        leaving.wait()


def proj_forward(att, x, valid, vectors, sources, table, row, rows):
    m, d = x.shape
    block = pl.BlockSpec((rows, d), lambda i, *_: (i, 0))
    return call(
        functools.partial(proj_kernel, row),
        (m // rows,),
        [block, block, pl.BlockSpec((rows, 1), lambda i, *_: (i, 0)), whole(VECTORS, d)]
        + [ANY] * len(sources),
        [
            ((m, d), F32, block),
            ((m, d), BF16, block),
            ((PLACES, d // PLACES, d), BF16, ANY),
        ],
        (att, x, valid, vectors, *sources),
        2 * m * d * d,
        [
            pltpu.VMEM((PLACES, d // PLACES, d), BF16),
            pltpu.SemaphoreType.DMA((PLACES,)),
            pltpu.SemaphoreType.DMA,
        ],
        (table,),
    )


def fc1_kernel(table, x_ref, bias_ref, *refs):
    sources = refs[:-6]
    act_ref, slope_ref, w_out, held, sems, leave = refs[-6:]
    step = pl.program_id(0)
    leaving = pltpu.make_async_copy(held, w_out, leave)

    @pl.when(step == 0)
    def _():
        copies = fetches(table, sources, 0, held.shape[1], held, sems)
        _starts(copies)
        _waits(copies)
        leaving.start()

    v = nt(x_ref[...], step_rows(held, step, act_ref.shape[1])) + bias_ref[...]
    share = 0.5 + 0.5 * lax.erf(v * (0.5**0.5))
    act_ref[...] = (v * share).astype(BF16)
    slope = share + v * (jnp.exp(-0.5 * v * v) * ((2 * np.pi) ** -0.5))
    slope_ref[...] = slope.astype(BF16)

    @pl.when(step == pl.num_programs(0) - 1)
    def _():
        leaving.wait()


def fc1_forward(x, bias, sources, table):
    m, d = x.shape
    f = bias.shape[1]
    rows = f // PLACES
    block = pl.BlockSpec((m, STEP), lambda i, *_: (0, i))
    return call(
        fc1_kernel,
        (f // STEP,),
        [whole(m, d), pl.BlockSpec((1, STEP), lambda i, *_: (0, i))] + [ANY] * len(sources),
        [
            ((m, f), BF16, block),
            ((m, f), BF16, block),
            ((PLACES, rows, d), BF16, ANY),
        ],
        (x, bias, *sources),
        2 * m * d * f,
        [
            pltpu.VMEM((PLACES, rows, d), BF16),
            pltpu.SemaphoreType.DMA((PLACES,)),
            pltpu.SemaphoreType.DMA,
        ],
        (table,),
    )


def fc2_kernel(x_ref, w_ref, vector_ref, hidden_ref, valid_ref, out_ref):
    branch = nt(x_ref[...], w_ref[...]) + vector_ref[FC2 : FC2 + 1]
    out_ref[...] = (hidden_ref[...] + valid_ref[...] * branch).astype(BF16)


def fc2_forward(x, w, vectors, hidden, valid):
    m, f = x.shape
    d = w.shape[0]
    step = 256
    return call(
        fc2_kernel,
        (d // step,),
        [whole(m, f), tall(step, f), cols(VECTORS, step), cols(m, step), whole(m, 1)],
        [((m, d), BF16, cols(m, step))],
        (x, w, vectors, hidden, valid),
        2 * m * d * f,
    )[0]


def fc2_weight_kernel(where_ref, grad_ref, act_ref, mine_ref, theirs_ref, sum_ref, held):
    @pl.when(pl.program_id(0) == 0)
    def _():
        sum_ref[...] = column_sum(grad_ref[...].astype(F32))

    held[...] = tn(grad_ref[...], act_ref[...]).astype(BF16)
    core = where_ref[PLACES]
    rows = mine_ref.shape[1]
    for chip in range(PLACES // 2):
        for out_ref, side in ((mine_ref, core), (theirs_ref, 1 - core)):
            place = 2 * chip + side
            at = pl.multiple_of(place * rows, rows)
            out_ref[where_ref[place]] = held[pl.ds(at, rows)]


def fc2_weight_grad(grad, act, where):
    m, d = grad.shape
    f = act.shape[1]
    half, rows = PLACES // 2, d // PLACES
    block = pl.BlockSpec((half, rows, STEP), lambda i, *_: (0, 0, i))
    return call(
        fc2_weight_kernel,
        (f // STEP,),
        [whole(m, d), pl.BlockSpec((m, STEP), lambda i, *_: (0, i))],
        [
            ((half, rows, f), BF16, block),
            ((half, rows, f), BF16, block),
            ((1, d), F32, whole(1, d)),
        ],
        (grad, act),
        2 * m * d * f,
        [pltpu.VMEM((d, STEP), BF16)],
        (where,),
    )


def pre_kernel(rows, table, where_ref, grad_ref, slope_ref, normed_ref, *refs):
    sources = refs[:-10]
    pre_ref, sum_ref, mine, theirs, w_out = refs[-10:-5]
    held, sems, leave, parts, part_sems = refs[-5:]
    step = pl.program_id(0)
    size = slope_ref.shape[1]
    leaving = pltpu.make_async_copy(held, w_out, leave)

    @pl.when(step == 0)
    def _():
        copies = fetches(table, sources, 0, held.shape[1], held, sems)
        _starts(copies)
        _waits(copies)
        leaving.start()

    at = pl.multiple_of(step * size, size)
    w = held[:, :, pl.ds(at, size)].reshape(grad_ref.shape[1], size)
    pre = (nn(grad_ref[...], w) * slope_ref[...].astype(F32)).astype(BF16)
    pre_ref[...] = pre
    sum_ref[...] = column_sum(pre.astype(F32))
    shares(tn(pre, normed_ref[...]), 0, rows, where_ref, parts, part_sems, mine, theirs)

    @pl.when(step == pl.num_programs(0) - 1)
    def _():
        leaving.wait()


def pre_backward(grad, slope, normed, sources, table, where, extra):
    m, d = grad.shape
    f = slope.shape[1]
    half, rows = PLACES // 2, f // PLACES
    block = pl.BlockSpec((m, STEP), lambda i, *_: (0, i))
    return call(
        functools.partial(pre_kernel, rows),
        (f // STEP,),
        [whole(m, d), block, whole(m, d)] + [ANY] * len(sources),
        [
            ((m, f), BF16, block),
            ((1, f), F32, pl.BlockSpec((1, STEP), lambda i, *_: (0, i))),
            ((half, rows + extra, d), BF16, ANY),
            ((half, rows + extra, d), BF16, ANY),
            ((PLACES, d // PLACES, f), BF16, ANY),
        ],
        (grad, slope, normed, *sources),
        4 * m * d * f,
        [
            pltpu.VMEM((PLACES, d // PLACES, f), BF16),
            pltpu.SemaphoreType.DMA((PLACES,)),
            pltpu.SemaphoreType.DMA,
            pltpu.VMEM((2, STEP, d), BF16),
            pltpu.SemaphoreType.DMA((2, STEP // rows)),
        ],
        (table, where),
    )


def second_norm_kernel(
    pre_ref, w_ref, hidden_ref, cot_ref, valid_ref, vector_ref,
    grad_ref, branch_ref, gain_sum_ref, shift_sum_ref, bias_sum_ref, acc_ref,
):
    step = pl.program_id(0)
    part = nn(pre_ref[...], w_ref[...])

    @pl.when(step == 0)
    def _():
        acc_ref[...] = part

    @pl.when(step > 0)
    def _():
        acc_ref[...] += part

    @pl.when(step == pl.num_programs(0) - 1)
    def _():
        grad = acc_ref[...]
        normal, inverse = centre(hidden_ref[...])
        gain_sum_ref[...] = column_sum(grad * normal)
        shift_sum_ref[...] = column_sum(grad)
        out = cot_ref[...].astype(F32) + norm_back(
            grad, normal, inverse, vector_ref[GAIN_TWO : GAIN_TWO + 1]
        )
        grad_ref[...] = out
        branch = (valid_ref[...] * out).astype(BF16)
        branch_ref[...] = branch
        bias_sum_ref[...] = column_sum(branch.astype(F32))


def second_norm_backward(pre, w, hidden, cot, valid, vectors):
    m, f = pre.shape
    d = w.shape[1]
    step = 2 * STEP
    return call(
        second_norm_kernel,
        (f // step,),
        [cols(m, step), tall(step, d), whole(m, d), whole(m, d), whole(m, 1), whole(VECTORS, d)],
        [((m, d), F32, whole(m, d)), ((m, d), BF16, whole(m, d))]
        + [((1, d), F32, whole(1, d))] * 3,
        (pre, w, hidden, cot, valid, vectors),
        2 * m * d * f,
        [pltpu.VMEM((m, d), F32)],
    )


def proj_back_kernel(row, where_ref, branch_ref, block_ref, att_ref, w_ref, *refs):
    grad_ref, mine, theirs, parts, part_sems = refs[2:]
    grad_ref[...] = nn(branch_ref[...], w_ref[...]).astype(BF16)
    rows = w_ref.shape[0] // PLACES
    shares(
        tn(block_ref[...], att_ref[...]), row, rows, where_ref, parts, part_sems, mine, theirs
    )


def proj_backward(branch, att, w, where, mine, theirs):
    m, d = branch.shape
    rows = d // PLACES
    block = pl.BlockSpec((m, STEP), lambda i, *_: (0, i))
    return call(
        functools.partial(proj_back_kernel, mine.shape[1] - rows),
        (d // STEP,),
        [whole(m, d), block, whole(m, d), pl.BlockSpec((d, STEP), lambda i, *_: (0, i)), ANY, ANY],
        [
            ((m, d), BF16, block),
            (mine.shape, BF16, ANY),
            (theirs.shape, BF16, ANY),
        ],
        (branch, branch, att, w, mine, theirs),
        4 * m * d * d,
        [pltpu.VMEM((2, STEP, d), BF16), pltpu.SemaphoreType.DMA((2, STEP // rows))],
        (where,),
        {5: 1, 6: 2},
    )


def attend_back_kernel(
    seg_col_ref, seg_row_ref, q_ref, k_ref, v_ref, total_ref, grad_ref, out_ref, bias_ref
):
    @pl.when(pl.program_id(0) == 0)
    def _():
        fill_bias(bias_ref, seg_col_ref, seg_row_ref)

    scaling = HDIM**-0.5
    k, v, grad = k_ref[...], v_ref[...], grad_ref[...]
    q = q_ref[...] * scaling
    low = lower_lanes(q.shape)
    bias = bias_ref[...]
    zero = jnp.zeros_like(q)
    sums = [0.0, 0.0, 0.0]
    for keep, lane in ((low, 0), (~low, HDIM)):
        q_own, k_own = jnp.where(keep, q, zero), jnp.where(keep, k, zero)
        grad_own = jnp.where(keep, grad, zero)
        probs = jnp.exp(nt(q_own, k) + bias - total_ref[:, lane : lane + 1])
        grad_probs = nt(grad_own, v)
        inner = jnp.sum(probs * grad_probs, axis=-1, keepdims=True)
        grad_scores = (probs * (grad_probs - inner)).astype(BF16)
        sums[0] += nn(grad_scores, k_own)
        sums[1] += tn(grad_scores, q_own)
        sums[2] += tn(probs.astype(BF16), grad_own)
    size = q.shape[1]
    for third, value in enumerate((sums[0] * scaling, sums[1], sums[2])):
        at = third * (out_ref.shape[1] // 3) + pl.program_id(0) * size
        out_ref[:, pl.ds(pl.multiple_of(at, size), size)] = value.astype(BF16)


def attend_backward(seg_col, seg_row, qkv, totals, grad, rows, which):
    d = qkv.shape[1] // 3
    pairs = d // (2 * HDIM)

    def block(offset):
        return pl.BlockSpec((rows, 2 * HDIM), lambda h: (which, offset + h))

    return call(
        attend_back_kernel,
        (pairs,),
        [
            pl.BlockSpec((rows, 1), lambda h: (which, 0)),
            pl.BlockSpec((1, 1, rows), lambda h: (which, 0, 0)),
            block(0),
            block(pairs),
            block(2 * pairs),
            block(0),
            block(0),
        ],
        [((rows, 3 * d), BF16, whole(rows, 3 * d))],
        (seg_col, seg_row, qkv, qkv, qkv, totals, grad),
        10 * rows * rows * d * 2,
        [pltpu.VMEM((rows, rows), F32)],
    )[0]


def qkv_weight_kernel(micro, rows, where_ref, *refs):
    grads, normed_ref = refs[:micro], refs[micro]
    sum_ref, mine, theirs, parts, part_sems = refs[micro + 1 :]
    total, sums = 0.0, 0.0
    m = normed_ref.shape[0] // micro
    for b, grad_ref in enumerate(grads):
        grad = grad_ref[...]
        sums += column_sum(grad.astype(F32))
        total += tn(grad, normed_ref[b * m : (b + 1) * m])
    sum_ref[...] = sums
    shares(total, 0, rows, where_ref, parts, part_sems, mine, theirs)


def qkv_weight_grad(grads, normed, where):
    m, d = normed.shape
    half, rows = PLACES // 2, 3 * d // PLACES
    step = 8 * rows
    block = pl.BlockSpec((grads[0].shape[0], step), lambda i, *_: (0, i))
    return call(
        functools.partial(qkv_weight_kernel, len(grads), rows),
        (3 * d // step,),
        [block] * len(grads) + [whole(m, d)],
        [
            ((1, 3 * d), F32, pl.BlockSpec((1, step), lambda i, *_: (0, i))),
            ((half, rows, d), BF16, ANY),
            ((half, rows, d), BF16, ANY),
        ],
        (*grads, normed),
        6 * m * d * d,
        [pltpu.VMEM((2, step, d), BF16), pltpu.SemaphoreType.DMA((2, 8))],
        (where,),
    )


def first_norm_kernel(micro, *refs):
    grads = refs[:micro]
    w_ref, x_ref, hidden_ref, vector_ref = refs[micro : micro + 4]
    out_ref, gain_sum_ref, shift_sum_ref, acc_ref = refs[micro + 4 :]
    step = pl.program_id(0)
    rows = grads[0].shape[0]
    for b, grad_ref in enumerate(grads):
        at = pl.ds(b * rows, rows)
        part = nn(grad_ref[...], w_ref[...])

        @pl.when(step == 0)
        def _():
            acc_ref[at] = part

        @pl.when(step > 0)
        def _():
            acc_ref[at] += part

    @pl.when(step == pl.num_programs(0) - 1)
    def _():
        grad = acc_ref[...]
        normal, inverse = centre(x_ref[...].astype(F32))
        gain_sum_ref[...] = column_sum(grad * normal)
        shift_sum_ref[...] = column_sum(grad)
        gain = vector_ref[GAIN_ONE : GAIN_ONE + 1]
        out_ref[...] = hidden_ref[...] + norm_back(grad, normal, inverse, gain)


def first_norm_backward(grads, w, x, grad_hidden, vectors):
    m, d = x.shape
    rows = grads[0].shape[0]
    step = 3 * d // 3
    return call(
        functools.partial(first_norm_kernel, len(grads)),
        (3 * d // step,),
        [cols(rows, step)] * len(grads)
        + [tall(step, d), whole(m, d), whole(m, d), whole(VECTORS, d)],
        [((m, d), F32, whole(m, d))] + [((1, d), F32, whole(1, d))] * 2,
        (*grads, w, x, grad_hidden, vectors),
        6 * m * d * d,
        [pltpu.VMEM((m, d), F32)],
    )


def padded(rows):
    return -(-rows // 16) * 16


def pad_rows(value, rows):
    return jnp.pad(value, ((0, 0),) * (value.ndim - 2) + ((0, rows - value.shape[-2]), (0, 0)))


def body(
    grid,
    tokens,
    segment_ids,
    cotangent,
    norm1_gain,
    norm1_bias,
    qkv_weight,
    qv_bias,
    proj_weight,
    proj_bias,
    norm2_gain,
    norm2_bias,
    fc1_weight,
    fc1_bias,
    fc2_weight,
    fc2_bias,
):
    micro, rows, width = tokens.shape
    n = grid.count
    all_rows = micro * rows
    me = lax.axis_index(AXIS)
    table = lax.dynamic_index_in_dim(jnp.asarray(grid.table()), me, 0, keepdims=False)
    smalls = (
        norm1_gain,
        norm1_bias,
        qv_bias,
        proj_bias,
        norm2_gain,
        norm2_bias,
        fc1_bias,
        fc2_bias,
    )
    sizes = [v.shape[0] for v in smalls]
    r_qkv, r_proj, r_fc1 = (w.shape[1] for w in (qkv_weight, proj_weight, fc1_weight))
    r_fc2 = fc2_weight.shape[1]
    direct = n == PLACES
    splits_one = [padded(r_qkv), 8]
    splits_two = [padded(r_fc1), padded(r_proj)]

    shard_one = first_shard(pad_rows(qkv_weight.T, splits_one[0]), smalls)
    line_one = gather_line(grid, shard_one)
    shard_two = jnp.concatenate(
        [pad_rows(fc1_weight.T, splits_two[0]), pad_rows(proj_weight.T, splits_two[1])]
    )
    x = tokens.reshape(all_rows, width)
    cot = cotangent.reshape(all_rows, width)
    seg_col = segment_ids.reshape(all_rows, 1)
    seg_row = segment_ids.reshape(micro, 1, rows)
    valid = (seg_col >= 0).astype(F32)
    grad_mlp = jnp.where(valid > 0, cot, 0)
    shard_two, table, seg_col, seg_row, valid, grad_mlp = lax.optimization_barrier(
        (shard_two, table, seg_col, seg_row, valid, grad_mlp)
    )
    line_two = gather_line(grid, shard_two)
    line_three = gather_line(grid, fc2_weight.T)
    parts_one = gather_sides(grid, line_one)
    parts_two = gather_sides(grid, line_two)
    parts_three = gather_sides(grid, line_three)
    if direct:
        places = small_places = table
        where = jnp.asarray(grid.where())[me]
        qkv_parts = small_parts = parts_one
        fc1_parts = proj_parts = parts_two
        proj_row = r_fc1
    else:
        qkv_all, small_all = put_in_order(parts_one, table, splits_one)
        fc1_all, proj_all = put_in_order(parts_two, table, splits_two)
        (fc2_all,) = put_in_order(parts_three, table, [r_fc2])
        places = jnp.arange(PLACES, dtype=jnp.int32)
        small_places = jnp.arange(n, dtype=jnp.int32)
        where = jnp.concatenate([places // 2, jnp.zeros((1,), jnp.int32)])
        qkv_parts = [qkv_all[:, :r_qkv].reshape(PLACES, -1, width)]
        small_parts = [small_all]
        fc1_parts = [fc1_all[:, :r_fc1].reshape(PLACES, -1, width)]
        proj_parts = [proj_all[:, :r_proj].reshape(PLACES, -1, width)]
        parts_three = [fc2_all.reshape(PLACES, -1, fc2_all.shape[2])]
        proj_row = 0

    normed_one, qkv, vectors, fc1_b, qkv_t = qkv_forward(
        x, qkv_parts, places, small_parts, small_places, sizes
    )
    attended, totals = attend(seg_col, seg_row, qkv, rows)
    hidden, normed_two, proj_t = proj_forward(
        attended, x, valid, vectors, proj_parts, places, proj_row, rows
    )
    activated, slope, fc1_t = fc1_forward(normed_two, fc1_b, fc1_parts, places)

    def reduce_group(mine, theirs, pieces):
        if not direct:
            ordered = jnp.stack([mine, theirs], axis=1).reshape(PLACES, *mine.shape[1:])
            cut, at = [], 0
            for own, kept in pieces:
                part = ordered[:, at : at + own * n // PLACES]
                cut.append(pad_rows(part.reshape(n, own, -1), kept))
                at += own * n // PLACES
            mine, theirs = pack(cut, table, grid.half)
        return scatter_sum(grid, mine, theirs)

    mine, theirs, grad_fc2_b = fc2_weight_grad(grad_mlp, activated, where)
    share_fc2 = reduce_group(mine, theirs, [(r_fc2, r_fc2)])
    grad_pre, grad_fc1_b, mine, theirs, fc2_t = pre_backward(
        grad_mlp, slope, normed_two, parts_three, places, where, width // PLACES
    )
    grad_hidden, grad_branch, grad_gain_two, grad_shift_two, grad_proj_b = (
        second_norm_backward(
            grad_pre, fc1_t.reshape(-1, width), hidden, cot, valid, vectors
        )
    )
    grad_att, mine, theirs = proj_backward(
        grad_branch, attended, proj_t.reshape(width, width), where, mine, theirs
    )
    share_two = reduce_group(mine, theirs, [(r_fc1, splits_two[0]), (r_proj, splits_two[1])])
    grad_qkv = [
        attend_backward(seg_col, seg_row, qkv, totals, grad_att, rows, b)
        for b in range(micro)
    ]
    sums, mine, theirs = qkv_weight_grad(grad_qkv, normed_one, where)
    share_one = reduce_group(mine, theirs, [(r_qkv, splits_one[0])])
    input_grad, grad_gain_one, grad_shift_one = first_norm_backward(
        grad_qkv, qkv_t.reshape(-1, width), x, grad_hidden, vectors
    )
    output = fc2_forward(
        activated, fc2_t.reshape(width, -1), vectors, hidden, valid
    )

    small_grads = jnp.concatenate(
        [
            grad_gain_one,
            grad_shift_one,
            sums[:, :width],
            sums[:, 2 * width :],
            grad_proj_b,
            grad_gain_two,
            grad_shift_two,
            grad_fc1_b.reshape(-1, width),
            grad_fc2_b,
            jnp.zeros((VECTORS - FC2 - 1, width), F32),
        ]
    )
    small_grads = sum_everywhere(grid, small_grads)
    own, row = [], 0
    for size in sizes:
        at = me * size
        place = (row + at // width, at % width)
        own.append(lax.dynamic_slice(small_grads, place, (1, size)).reshape(size))
        row += -(-size * n // width)
    s_gain_one, s_shift_one, s_qv, s_proj, s_gain_two, s_shift_two, s_fc1, s_fc2 = own
    return (
        output.reshape(micro, rows, width),
        input_grad.reshape(micro, rows, width),
        s_gain_one,
        s_shift_one,
        share_one[:r_qkv].T,
        s_qv,
        share_two[splits_two[0] : splits_two[0] + r_proj].T,
        s_proj,
        s_gain_two,
        s_shift_two,
        share_two[:r_fc1].T,
        s_fc1,
        share_fc2.T,
        s_fc2,
    )


def solution(mesh):
    row = P(None, AXIS, None)
    vec = P(AXIS)
    mat = P(None, AXIS)
    grid = Grid(mesh.size)

    def layer(*args):
        return body(grid, *args)

    return jax.shard_map(
        layer,
        mesh=mesh,
        in_specs=(row, mat, row) + (vec, vec, mat, vec, mat, vec) * 2,
        out_specs=(row, row) + (vec, vec, mat, vec, mat, vec) * 2,
        check_vma=False,
    )
```

```python
import functools

import jax
import jax.numpy as jnp
import numpy as np
from jax import lax
from jax.experimental import pallas as pl
from jax.experimental.pallas import tpu as pltpu
from jax.sharding import PartitionSpec as P


HDIM = 64
AXIS = "fsdp"
BF16 = jnp.bfloat16
F32 = jnp.float32


class Grid:
    def __init__(self, count):
        self.count = count
        chips = count // 2
        if chips == 16:
            sizes, line = (4, 2, 2), 0
        elif chips == 128:
            sizes, line = (4, 4, 8), 2
        else:
            sizes, line = (chips, 1, 1), 0
        self.sizes = sizes
        self.line = line
        self.pair = tuple(a for a in range(3) if a != line)
        self.n_line = sizes[line]
        self.n_side = sizes[self.pair[0]]
        assert sizes[self.pair[0]] == sizes[self.pair[1]]
        self.half = chips

    def coords(self, index):
        core = index % 2
        chip = index // 2
        _, b, c = self.sizes
        return [chip // (b * c), (chip // c) % b, chip % c], core

    def index(self, where, core):
        a, b, c = self.sizes
        return ((where[0] % a * b + where[1] % b) * c + where[2] % c) * 2 + core

    def axis_of(self, phase, core):
        if phase == 0:
            return self.line
        return self.pair[(phase - 1) ^ core]

    def moved(self, index, phase, shift):
        where, core = self.coords(index)
        where[self.axis_of(phase, core)] += shift
        return self.index(where, core)

    def pairs(self, phase, shift):
        return [(i, self.moved(i, phase, shift)) for i in range(self.count)]

    def swap(self):
        return [(i, i ^ 1) for i in range(self.count)]

    def slots(self, me):
        where, core = self.coords(me)
        found = []
        for q in range(self.n_side):
            for p in range(self.n_side):
                for k in range(self.n_line):
                    there = list(where)
                    there[self.axis_of(2, core)] -= q
                    there[self.axis_of(1, core)] -= p
                    there[self.line] -= k
                    found.append(self.index(there, core))
        return found

    def table(self):
        return np.array(
            [self.slots(i) + self.slots(i ^ 1) for i in range(self.count)], np.int32
        )


    def where(self):
        table = self.table()
        found = np.zeros((self.count, self.count + 1), np.int32)
        for i in range(self.count):
            found[i, table[i]] = np.arange(self.count) % self.half
            found[i, -1] = i % 2
        return found


def _starts(copies):
    for copy in copies:
        copy.start()


def order_kernel(splits, counts, table, *refs):
    n_src = len(counts)
    sources = refs[:n_src]
    outs = refs[n_src : n_src + len(splits)]
    held, sem_in, sem_out = refs[n_src + len(splits) :]
    incoming, at = [], 0
    for k, size in enumerate(counts):
        incoming.append(
            pltpu.make_async_copy(sources[k], held.at[pl.ds(at, size)], sem_in.at[k])
        )
        at += size
    _starts(incoming)
    outgoing, at = [], 0
    for k, size in enumerate(counts):
        incoming[k].wait()
        for s in range(at, at + size):
            place = table[s]
            row = 0
            for o, rows in enumerate(splits):
                copy = pltpu.make_async_copy(
                    held.at[s, pl.ds(row, rows)], outs[o].at[place], sem_out.at[s, o]
                )
                copy.start()
                outgoing.append(copy)
                row += rows
        at += size
    for copy in outgoing:
        copy.wait()


def put_in_order(sources, table, splits):
    rows, width = sources[0].shape[-2:]
    counts = [s.shape[0] for s in sources]
    total = sum(counts)
    space = pl.BlockSpec(memory_space=pl.ANY)
    moved = 2 * 2 * total * rows * width
    return pl.pallas_call(
        functools.partial(order_kernel, tuple(splits), tuple(counts)),
        out_shape=[jax.ShapeDtypeStruct((total, r, width), BF16) for r in splits],
        grid_spec=pltpu.PrefetchScalarGridSpec(
            num_scalar_prefetch=1,
            grid=(),
            in_specs=[space] * len(sources),
            out_specs=[space] * len(splits),
            scratch_shapes=[
                pltpu.VMEM((total, rows, width), BF16),
                pltpu.SemaphoreType.DMA((len(sources),)),
                pltpu.SemaphoreType.DMA((total, len(splits))),
            ],
        ),
        cost_estimate=pl.CostEstimate(flops=0, bytes_accessed=moved, transcendentals=0),
    )(table, *sources)


def pack_kernel(splits, half, table, *refs):
    n_src = len(splits)
    sources = refs[:n_src]
    mine, theirs = refs[n_src : n_src + 2]
    held, sem_in, sem_out = refs[n_src + 2 :]
    incoming = []
    for s in list(range(half, 2 * half)) + list(range(half)):
        place = table[s]
        row, copies = 0, []
        for o, rows in enumerate(splits):
            copy = pltpu.make_async_copy(
                sources[o].at[place], held.at[s, pl.ds(row, rows)], sem_in.at[s, o]
            )
            copy.start()
            copies.append(copy)
            row += rows
        incoming.append((s, copies))
    for s, copies in incoming:
        for copy in copies:
            copy.wait()
        if s == 2 * half - 1:
            pltpu.make_async_copy(
                held.at[pl.ds(half, half)], theirs, sem_out.at[1]
            ).start()
        if s == half - 1:
            pltpu.make_async_copy(held.at[pl.ds(0, half)], mine, sem_out.at[0]).start()
    pltpu.make_async_copy(held.at[pl.ds(half, half)], theirs, sem_out.at[1]).wait()
    pltpu.make_async_copy(held.at[pl.ds(0, half)], mine, sem_out.at[0]).wait()


def pack(sources, table, half):
    splits = [s.shape[1] for s in sources]
    rows, width = sum(splits), sources[0].shape[2]
    space = pl.BlockSpec(memory_space=pl.ANY)
    moved = 2 * 2 * 2 * half * rows * width
    return pl.pallas_call(
        functools.partial(pack_kernel, tuple(splits), half),
        out_shape=[jax.ShapeDtypeStruct((half, rows, width), BF16)] * 2,
        grid_spec=pltpu.PrefetchScalarGridSpec(
            num_scalar_prefetch=1,
            grid=(),
            in_specs=[space] * len(sources),
            out_specs=[space] * 2,
            scratch_shapes=[
                pltpu.VMEM((2 * half, rows, width), BF16),
                pltpu.SemaphoreType.DMA((2 * half, len(splits))),
                pltpu.SemaphoreType.DMA((2,)),
            ],
        ),
        cost_estimate=pl.CostEstimate(flops=0, bytes_accessed=moved, transcendentals=0),
    )(table, *sources)


def join_kernel(count, *refs):
    sources, out, held, sem_in, sem_out = refs[:count], *refs[count:]
    copies = []
    for k, source in enumerate(sources):
        copies.append(pltpu.make_async_copy(source, held.at[k], sem_in.at[k]))
    _starts(copies)
    leaving = []
    for k, copy in enumerate(copies):
        copy.wait()
        leaving.append(pltpu.make_async_copy(held.at[k], out.at[k], sem_out.at[k]))
        leaving[-1].start()
    for copy in leaving:
        copy.wait()


def join(pieces):
    count, shape = len(pieces), pieces[0].shape
    size = int(np.prod(shape))
    space = pl.BlockSpec(memory_space=pl.ANY)
    return pl.pallas_call(
        functools.partial(join_kernel, count),
        out_shape=jax.ShapeDtypeStruct((count, *shape), BF16),
        in_specs=[space] * count,
        out_specs=space,
        scratch_shapes=[
            pltpu.VMEM((count, *shape), BF16),
            pltpu.SemaphoreType.DMA((count,)),
            pltpu.SemaphoreType.DMA((count,)),
        ],
        cost_estimate=pl.CostEstimate(
            flops=0, bytes_accessed=4 * count * size, transcendentals=0
        ),
    )(*pieces)


def first_shard_kernel(w_ref, *refs):
    smalls, out_ref = refs[:-1], refs[-1]
    rows = w_ref.shape[0]
    out_ref[:rows] = w_ref[...]
    out_ref[rows:] = jnp.zeros((out_ref.shape[0] - rows, out_ref.shape[1]), BF16)
    at = 0
    for small in smalls:
        size = small.shape[1]
        out_ref[rows : rows + 1, at : at + size] = small[...]
        at += size


def first_shard(w, smalls):
    rows, width = w.shape
    return pl.pallas_call(
        first_shard_kernel,
        out_shape=jax.ShapeDtypeStruct((rows + 8, width), BF16),
        name="first_shard",
    )(w, *[v.reshape(1, -1) for v in smalls])


def send(value, pairs):
    return lax.ppermute(value, AXIS, pairs)


def gather_line(grid, shard, also=None):
    got = [shard]
    for k in range(1, grid.n_line):
        got.append(send(shard, grid.pairs(0, k)))
    if also is not None:
        got, also = lax.optimization_barrier((got, also))
    line = join(got)
    return line if also is None else (line, also)


def gather_sides(grid, block):
    n = grid.n_side
    near = [block]
    for k in range(1, n):
        near.append(send(block, grid.pairs(1, k)))
    near = join(near).reshape(-1, *block.shape[1:])
    far = [send(near, grid.pairs(2, k)) for k in range(1, n)]
    back = [send(near, grid.swap())]
    for k, part in enumerate(far, 1):
        back.append(send(part, grid.swap()))
    return [near] + far + back


def scatter_sum(grid, mine, theirs):
    n, line = grid.n_side, grid.n_line
    arrived = send(theirs, grid.swap())
    shape = (n, n, line) + mine.shape[1:]
    terms = [mine.reshape(shape), arrived.reshape(shape)]
    for phase in (2, 1, 0):
        size = terms[0].shape[0]
        got = []
        for k in range(1, size):
            part = sum(t[k].astype(F32) for t in terms).astype(BF16)
            got.append(send(part, grid.pairs(phase, -k)))
        terms = [t[0] for t in terms] + got
    return sum(t.astype(F32) for t in terms)


def sum_everywhere(grid, value):
    value += send(value, grid.swap())
    for phase in (2, 1, 0):
        size = grid.n_line if phase == 0 else grid.n_side
        value += sum(send(value, grid.pairs(phase, k)) for k in range(1, size))
    return value


def nt(a, b):
    return lax.dot_general(a, b, (((1,), (1,)), ((), ())), preferred_element_type=F32)


def nn(a, b):
    return lax.dot_general(a, b, (((1,), (0,)), ((), ())), preferred_element_type=F32)


def tn(a, b):
    return lax.dot_general(a, b, (((0,), (0,)), ((), ())), preferred_element_type=F32)


def centre(values):
    average = jnp.mean(values, axis=-1, keepdims=True)
    centred = values - average
    spread = jnp.mean(centred * centred, axis=-1, keepdims=True)
    inverse = lax.rsqrt(spread + 1e-06)
    return centred * inverse, inverse


def norm_back(grad, normal, inverse, gain):
    scaled = grad * gain
    first = jnp.mean(scaled, axis=-1, keepdims=True)
    second = jnp.mean(scaled * normal, axis=-1, keepdims=True)
    return inverse * (scaled - first - normal * second)


def column_sum(values):
    return jnp.sum(values, axis=0, keepdims=True)


def whole(*shape):
    return pl.BlockSpec(shape, lambda *_: (0,) * len(shape))


def cols(rows, width):
    return pl.BlockSpec((rows, width), lambda i: (0, i))


def tall(rows, width):
    return pl.BlockSpec((rows, width), lambda i: (i, 0))


def call(kernel, grid, ins, outs, args, flops, scratch=(), tables=(), aliases=None):
    shapes = [jax.ShapeDtypeStruct(s, d) for s, d, _ in outs]
    size = sum(np.prod(a.shape) * a.dtype.itemsize for a in list(args) + shapes)
    return pl.pallas_call(
        kernel,
        out_shape=shapes,
        grid_spec=pltpu.PrefetchScalarGridSpec(
            num_scalar_prefetch=len(tables),
            grid=grid,
            in_specs=ins,
            out_specs=[o[2] for o in outs],
            scratch_shapes=list(scratch),
        ),
        input_output_aliases=aliases or {},
        cost_estimate=pl.CostEstimate(
            flops=int(flops), bytes_accessed=int(size), transcendentals=0
        ),
    )(*tables, *args)


def fetches(table, sources, row, rows, held, sems):
    copies, at = [], 0
    for source in sources:
        for s in range(source.shape[0]):
            copies.append(
                pltpu.make_async_copy(
                    source.at[s, pl.ds(row, rows)], held.at[table[at]], sems.at[at]
                )
            )
            at += 1
    return copies


def _waits(copies):
    for copy in copies:
        copy.wait()


def step_rows(held_ref, step, size):
    rows, width = held_ref.shape[1:]
    count = size // rows
    return held_ref[pl.ds(step * count, count)].reshape(size, width)


def share_out(place, row, rows, where_ref, held_ref, sems, mine, theirs, core):
    for j in range(held_ref.shape[0] // rows):
        slot = where_ref[place + j]
        source = held_ref.at[pl.ds(j * rows, rows)]
        for out, own in ((mine, True), (theirs, False)):

            @pl.when((core == j % 2) == own)
            def _():
                pltpu.make_async_copy(
                    source, out.at[slot, pl.ds(row, rows)], sems.at[j]
                ).start()


def shared_out(row, rows, held_ref, sems, mine):
    for j in range(held_ref.shape[0] // rows):
        source = held_ref.at[pl.ds(j * rows, rows)]
        pltpu.make_async_copy(source, mine.at[0, pl.ds(row, rows)], sems.at[j]).wait()


def shares(result, row, rows, where_ref, held_ref, sems, mine, theirs):
    step, last = pl.program_id(0), pl.num_programs(0) - 1
    now = step % 2
    count = held_ref.shape[1] // rows
    core = where_ref[where_ref.shape[0] - 1]

    @pl.when(step >= 2)
    def _():
        shared_out(row, rows, held_ref.at[now], sems.at[now], mine)

    held_ref[now] = result.astype(BF16)
    share_out(
        step * count, row, rows, where_ref, held_ref.at[now], sems.at[now],
        mine, theirs, core,
    )

    @pl.when(step == last)
    def _():
        shared_out(row, rows, held_ref.at[now], sems.at[now], mine)
        if pl.num_programs(0) > 1:
            shared_out(row, rows, held_ref.at[1 - now], sems.at[1 - now], mine)


ANY = pl.BlockSpec(memory_space=pl.ANY)
PLACES = 32


STEP = 512


GAIN_ONE, SHIFT_ONE, QV, PROJ, GAIN_TWO, SHIFT_TWO, FC2, VECTORS = 0, 1, 2, 4, 5, 6, 11, 16


def spread(piece, width):
    devices, size = piece.shape
    lane = lax.broadcasted_iota(jnp.int32, (size, width), 1)
    entry = lax.broadcasted_iota(jnp.int32, (size, width), 0)
    copied = nn(piece, (lane % size == entry).astype(BF16))
    device = lax.broadcasted_iota(jnp.int32, (devices, width), 0)
    owner = lax.broadcasted_iota(jnp.int32, (devices, width), 1) // size
    per_row = width // size
    return [
        column_sum(jnp.where(device - row * per_row == owner, copied, 0.0))
        for row in range(-(-devices * size // width))
    ]


def qkv_kernel(n_src, sizes, table, small_table, x_ref, *refs):
    sources, smalls = refs[:n_src], refs[n_src : -10]
    normed_ref, out_ref, vector_ref, fc1_ref, w_out = refs[-10:-5]
    held, small_held, bias_ref, sems, small_sems = refs[-5:]
    step = pl.program_id(0)
    _, width = x_ref.shape
    rows = held.shape[1]
    leaving = pltpu.make_async_copy(held, w_out, small_sems.at[small_held.shape[0]])

    @pl.when(step == 0)
    def _():
        small_copies = fetches(small_table, smalls, smalls[0].shape[1] - 8, 8, small_held, small_sems)
        copies = fetches(table, sources, 0, rows, held, sems)
        _starts(small_copies)
        _starts(copies)
        normal, _ = centre(x_ref[...].astype(F32))
        _waits(small_copies)
        values = small_held[:, 0, :]
        at, row = 0, 0
        vector_ref[...] = jnp.zeros(vector_ref.shape, F32)
        for number, size in enumerate(sizes):
            for k, line in enumerate(spread(values[:, at : at + size], width)):
                vector_ref[row : row + 1] = line
                if number == 6:
                    fc1_ref[:, k * width : (k + 1) * width] = line
                row += 1
            at += size
        bias_ref[:, :width] = vector_ref[QV : QV + 1]
        bias_ref[:, width : 2 * width] = jnp.zeros((1, width), F32)
        bias_ref[:, 2 * width :] = vector_ref[QV + 1 : QV + 2]
        gain, shift = vector_ref[GAIN_ONE : GAIN_ONE + 1], vector_ref[SHIFT_ONE : SHIFT_ONE + 1]
        normed_ref[...] = (normal * gain + shift).astype(BF16)
        _waits(copies)
        leaving.start()

    size = out_ref.shape[1]
    bias = bias_ref[:, pl.ds(pl.multiple_of(step * size, size), size)]
    out_ref[...] = (nt(normed_ref[...], step_rows(held, step, size)) + bias).astype(BF16)

    @pl.when(step == pl.num_programs(0) - 1)
    def _():
        leaving.wait()


def qkv_forward(x, sources, table, smalls, small_table, sizes):
    m, d = x.shape
    n = 3 * d
    rows = n // PLACES
    step = 8 * rows
    devices = sum(s.shape[0] for s in smalls)
    ff = sizes[6] * devices
    return call(
        functools.partial(qkv_kernel, len(sources), tuple(sizes)),
        (n // step,),
        [whole(m, d)] + [ANY] * (len(sources) + len(smalls)),
        [
            ((m, d), BF16, whole(m, d)),
            ((m, n), BF16, pl.BlockSpec((m, step), lambda i, *_: (0, i))),
            ((VECTORS, d), F32, whole(VECTORS, d)),
            ((1, ff), F32, whole(1, ff)),
            ((PLACES, rows, d), BF16, ANY),
        ],
        (x, *sources, *smalls),
        2 * m * d * n,
        [
            pltpu.VMEM((PLACES, rows, d), BF16),
            pltpu.VMEM((devices, 8, d), BF16),
            pltpu.VMEM((1, n), F32),
            pltpu.SemaphoreType.DMA((PLACES,)),
            pltpu.SemaphoreType.DMA((devices + 1,)),
        ],
        (table, small_table),
    )


def fill_bias(bias_ref, seg_col_ref, seg_row_ref):
    seg_q, seg_k = seg_col_ref[...], seg_row_ref[0]
    rows = seg_q.shape[0]
    row = lax.broadcasted_iota(jnp.int32, (rows, rows), 0)
    col = lax.broadcasted_iota(jnp.int32, (rows, rows), 1)
    allowed = ((seg_q == seg_k) & (seg_k >= 0)) | (row == col)
    bias_ref[...] = jnp.where(allowed, 0.0, -1e30)


def lower_lanes(shape):
    return lax.broadcasted_iota(jnp.int32, shape, 1) < HDIM


def attend_kernel(seg_col_ref, seg_row_ref, q_ref, k_ref, v_ref, out_ref, total_ref, bias_ref):
    @pl.when(pl.program_id(1) == 0)
    def _():
        fill_bias(bias_ref, seg_col_ref, seg_row_ref)

    k, v = k_ref[...], v_ref[...]
    q = q_ref[...] * (HDIM**-0.5)
    low = lower_lanes(q.shape)
    bias = bias_ref[...]
    found, totals = [], []
    for keep in (low, ~low):
        scores = nt(jnp.where(keep, q, 0), k) + bias
        most = jnp.max(scores, axis=-1, keepdims=True)
        grown = jnp.exp(scores - most)
        total = jnp.sum(grown, axis=-1, keepdims=True)
        probs = (grown * (1.0 / total)).astype(BF16)
        found.append(nn(probs, v))
        totals.append(most + jnp.log(total))
    out_ref[...] = jnp.where(low, found[0], found[1]).astype(BF16)
    total_ref[...] = jnp.where(low, totals[0], totals[1])


def head_block(rows, offset):
    return pl.BlockSpec((rows, 2 * HDIM), lambda b, h: (b, offset + h))


def attend(seg_col, seg_row, qkv, rows):
    m, d = qkv.shape[0], qkv.shape[1] // 3
    pairs = d // (2 * HDIM)
    return call(
        attend_kernel,
        (m // rows, pairs),
        [
            pl.BlockSpec((rows, 1), lambda b, h: (b, 0)),
            pl.BlockSpec((1, 1, rows), lambda b, h: (b, 0, 0)),
            head_block(rows, 0),
            head_block(rows, pairs),
            head_block(rows, 2 * pairs),
        ],
        [((m, d), BF16, head_block(rows, 0)), ((m, d), F32, head_block(rows, 0))],
        (seg_col, seg_row, qkv, qkv, qkv),
        4 * m * rows * d * 2,
        [pltpu.VMEM((rows, rows), F32)],
    )


def mlp_kernel(row, part, table, where_ref, *refs):
    att_ref, x_ref, valid_ref, vector_ref, fc1_ref, grad_ref = refs[:6]
    n_src = (len(refs) - 21) // 2
    proj_parts, fc1_parts = refs[6 : 6 + n_src], refs[6 + n_src : 6 + 2 * n_src]
    hidden_ref, normed_ref, act_ref, slope_ref, mine_ref, theirs_ref, sum_ref = refs[-15:-8]
    proj_out, fc1_out, proj_held, fc1_held, proj_sems, fc1_sems, leave, held = refs[-8:]
    step = pl.program_id(0)
    leaving = [
        pltpu.make_async_copy(proj_held, proj_out, leave.at[0]),
        pltpu.make_async_copy(fc1_held, fc1_out, leave.at[1]),
    ]

    @pl.when(step == 0)
    def _():
        proj_copies = fetches(table, proj_parts, row, proj_held.shape[1], proj_held, proj_sems)
        fc1_copies = fetches(table, fc1_parts, 0, fc1_held.shape[1], fc1_held, fc1_sems)
        _starts(proj_copies)
        _starts(fc1_copies)
        sum_ref[...] = column_sum(grad_ref[...].astype(F32))
        _waits(proj_copies)
        leaving[0].start()
        width = x_ref.shape[1]
        w = step_rows(proj_held, 0, width)
        bias = vector_ref[PROJ : PROJ + 1]
        gain, shift = vector_ref[GAIN_TWO : GAIN_TWO + 1], vector_ref[SHIFT_TWO : SHIFT_TWO + 1]
        for at in range(0, x_ref.shape[0], 160):
            band = slice(at, at + 160)
            branch = nt(att_ref[band], w) + bias
            hidden = x_ref[band].astype(F32) + valid_ref[band] * branch
            hidden_ref[band] = hidden
            normal, _ = centre(hidden)
            normed_ref[band] = (normal * gain + shift).astype(BF16)
        _waits(fc1_copies)
        leaving[1].start()

    size = act_ref.shape[1]
    normed, grad = normed_ref[...], grad_ref[...]
    for at in range(0, size, part):
        w = step_rows(fc1_held, step * (size // part) + at // part, part)
        v = nt(normed, w) + fc1_ref[:, at : at + part]
        share = 0.5 + 0.5 * lax.erf(v * (0.5**0.5))
        act = (v * share).astype(BF16)
        act_ref[:, at : at + part] = act
        slope = share + v * (jnp.exp(-0.5 * v * v) * ((2 * np.pi) ** -0.5))
        slope_ref[:, at : at + part] = slope.astype(BF16)
        held[:, at : at + part] = tn(grad, act).astype(BF16)

    core = where_ref[PLACES]
    rows = mine_ref.shape[1]
    for chip in range(PLACES // 2):
        for out_ref, side in ((mine_ref, core), (theirs_ref, 1 - core)):
            place = 2 * chip + side
            at = pl.multiple_of(place * rows, rows)
            out_ref[where_ref[place]] = held[pl.ds(at, rows)]

    @pl.when(step == pl.num_programs(0) - 1)
    def _():
        for copy in leaving:
            copy.wait()


def mlp_forward(att, x, valid, vectors, fc1_b, grad, proj_parts, row, fc1_parts, table, where, step=1024, part=1024):
    m, d = x.shape
    f = fc1_b.shape[1]
    half, rows = PLACES // 2, d // PLACES
    block = pl.BlockSpec((m, step), lambda i, *_: (0, i))
    slots = pl.BlockSpec((half, rows, step), lambda i, *_: (0, 0, i))
    return call(
        functools.partial(mlp_kernel, row, part),
        (f // step,),
        [whole(m, d), whole(m, d), whole(m, 1), whole(VECTORS, d)]
        + [pl.BlockSpec((1, step), lambda i, *_: (0, i)), whole(m, d)]
        + [ANY] * (len(proj_parts) + len(fc1_parts)),
        [
            ((m, d), F32, whole(m, d)),
            ((m, d), BF16, whole(m, d)),
            ((m, f), BF16, block),
            ((m, f), BF16, block),
            ((half, rows, f), BF16, slots),
            ((half, rows, f), BF16, slots),
            ((1, d), F32, whole(1, d)),
            ((PLACES, rows, d), BF16, ANY),
            ((PLACES, f // PLACES, d), BF16, ANY),
        ],
        (att, x, valid, vectors, fc1_b, grad, *proj_parts, *fc1_parts),
        2 * m * d * d + 4 * m * d * f,
        [
            pltpu.VMEM((PLACES, rows, d), BF16),
            pltpu.VMEM((PLACES, f // PLACES, d), BF16),
            pltpu.SemaphoreType.DMA((PLACES,)),
            pltpu.SemaphoreType.DMA((PLACES,)),
            pltpu.SemaphoreType.DMA((2,)),
            pltpu.VMEM((d, step), BF16),
        ],
        (table, where),
    )


def fc2_kernel(x_ref, w_ref, vector_ref, hidden_ref, valid_ref, out_ref):
    branch = nt(x_ref[...], w_ref[...]) + vector_ref[FC2 : FC2 + 1]
    out_ref[...] = (hidden_ref[...] + valid_ref[...] * branch).astype(BF16)


def fc2_forward(x, w, vectors, hidden, valid):
    m, f = x.shape
    d = w.shape[0]
    step = 256
    return call(
        fc2_kernel,
        (d // step,),
        [whole(m, f), tall(step, f), cols(VECTORS, step), cols(m, step), whole(m, 1)],
        [((m, d), BF16, cols(m, step))],
        (x, w, vectors, hidden, valid),
        2 * m * d * f,
    )[0]


def mlp_back_kernel(rows, table, where_ref, *refs):
    grad_ref, slope_ref, normed_ref, w_ref, hidden_ref, cot_ref, valid_ref, vector_ref = refs[:8]
    sources = refs[8:-15]
    sum_ref, mine, theirs, w_out = refs[-15:-11]
    out_ref, branch_ref, gain_sum_ref, shift_sum_ref, bias_sum_ref = refs[-11:-6]
    acc_ref, held, sems, leave, parts, part_sems = refs[-6:]
    step, last = pl.program_id(0), pl.num_programs(0) - 1
    size = slope_ref.shape[1]
    leaving = pltpu.make_async_copy(held, w_out, leave)

    @pl.when(step == 0)
    def _():
        copies = fetches(table, sources, 0, held.shape[1], held, sems)
        _starts(copies)
        acc_ref[...] = jnp.zeros(acc_ref.shape, F32)
        _waits(copies)
        leaving.start()

    at = pl.multiple_of(step * size, size)
    w = held[:, :, pl.ds(at, size)].reshape(grad_ref.shape[1], size)
    pre = (nn(grad_ref[...], w) * slope_ref[...].astype(F32)).astype(BF16)
    sum_ref[...] = column_sum(pre.astype(F32))
    shares(tn(pre, normed_ref[...]), 0, rows, where_ref, parts, part_sems, mine, theirs)
    acc_ref[...] += nn(pre, w_ref[...])

    @pl.when(step == last)
    def _():
        gain_sum = shift_sum = bias_sum = 0.0
        gain = vector_ref[GAIN_TWO : GAIN_TWO + 1]
        for first in range(0, acc_ref.shape[0], 160):
            band = slice(first, first + 160)
            grad = acc_ref[band]
            normal, inverse = centre(hidden_ref[band])
            gain_sum += column_sum(grad * normal)
            shift_sum += column_sum(grad)
            out = cot_ref[band].astype(F32) + norm_back(grad, normal, inverse, gain)
            out_ref[band] = out
            branch = (valid_ref[band] * out).astype(BF16)
            branch_ref[band] = branch
            bias_sum += column_sum(branch.astype(F32))
        gain_sum_ref[...], shift_sum_ref[...], bias_sum_ref[...] = gain_sum, shift_sum, bias_sum
        leaving.wait()


def mlp_backward(grad, slope, normed, w, hidden, cot, valid, vectors, sources, table, where, extra, step=1024):
    m, d = grad.shape
    f = slope.shape[1]
    half, rows = PLACES // 2, f // PLACES
    block = pl.BlockSpec((m, step), lambda i, *_: (0, i))
    return call(
        functools.partial(mlp_back_kernel, rows),
        (f // step,),
        [whole(m, d), block, whole(m, d), pl.BlockSpec((step, d), lambda i, *_: (i, 0))]
        + [whole(m, d), whole(m, d), whole(m, 1), whole(VECTORS, d)]
        + [ANY] * len(sources),
        [
            ((1, f), F32, pl.BlockSpec((1, step), lambda i, *_: (0, i))),
            ((half, rows + extra, d), BF16, ANY),
            ((half, rows + extra, d), BF16, ANY),
            ((PLACES, d // PLACES, f), BF16, ANY),
            ((m, d), F32, whole(m, d)),
            ((m, d), BF16, whole(m, d)),
        ]
        + [((1, d), F32, whole(1, d))] * 3,
        (grad, slope, normed, w, hidden, cot, valid, vectors, *sources),
        6 * m * d * f,
        [
            pltpu.VMEM((m, d), F32),
            pltpu.VMEM((PLACES, d // PLACES, f), BF16),
            pltpu.SemaphoreType.DMA((PLACES,)),
            pltpu.SemaphoreType.DMA,
            pltpu.VMEM((2, step, d), BF16),
            pltpu.SemaphoreType.DMA((2, step // rows)),
        ],
        (table, where),
    )


def proj_back_kernel(row, where_ref, branch_ref, block_ref, att_ref, w_ref, *refs):
    grad_ref, mine, theirs, parts, part_sems = refs[2:]
    grad_ref[...] = nn(branch_ref[...], w_ref[...]).astype(BF16)
    rows = w_ref.shape[0] // PLACES
    shares(
        tn(block_ref[...], att_ref[...]), row, rows, where_ref, parts, part_sems, mine, theirs
    )


def proj_backward(branch, att, w, where, mine, theirs):
    m, d = branch.shape
    rows = d // PLACES
    block = pl.BlockSpec((m, STEP), lambda i, *_: (0, i))
    return call(
        functools.partial(proj_back_kernel, mine.shape[1] - rows),
        (d // STEP,),
        [whole(m, d), block, whole(m, d), pl.BlockSpec((d, STEP), lambda i, *_: (0, i)), ANY, ANY],
        [
            ((m, d), BF16, block),
            (mine.shape, BF16, ANY),
            (theirs.shape, BF16, ANY),
        ],
        (branch, branch, att, w, mine, theirs),
        4 * m * d * d,
        [pltpu.VMEM((2, STEP, d), BF16), pltpu.SemaphoreType.DMA((2, STEP // rows))],
        (where,),
        {5: 1, 6: 2},
    )


def attend_back_kernel(
    seg_col_ref, seg_row_ref, q_ref, k_ref, v_ref, total_ref, grad_ref, out_ref, bias_ref
):
    @pl.when(pl.program_id(0) == 0)
    def _():
        fill_bias(bias_ref, seg_col_ref, seg_row_ref)

    scaling = HDIM**-0.5
    k, v, grad = k_ref[...], v_ref[...], grad_ref[...]
    q = q_ref[...] * scaling
    low = lower_lanes(q.shape)
    bias = bias_ref[...]
    zero = jnp.zeros_like(q)
    sums = [0.0, 0.0, 0.0]
    for keep, lane in ((low, 0), (~low, HDIM)):
        q_own, k_own = jnp.where(keep, q, zero), jnp.where(keep, k, zero)
        grad_own = jnp.where(keep, grad, zero)
        probs = jnp.exp(nt(q_own, k) + bias - total_ref[:, lane : lane + 1])
        grad_probs = nt(grad_own, v)
        inner = jnp.sum(probs * grad_probs, axis=-1, keepdims=True)
        grad_scores = (probs * (grad_probs - inner)).astype(BF16)
        sums[0] += nn(grad_scores, k_own)
        sums[1] += tn(grad_scores, q_own)
        sums[2] += tn(probs.astype(BF16), grad_own)
    size = q.shape[1]
    for third, value in enumerate((sums[0] * scaling, sums[1], sums[2])):
        at = third * (out_ref.shape[1] // 3) + pl.program_id(0) * size
        out_ref[:, pl.ds(pl.multiple_of(at, size), size)] = value.astype(BF16)


def attend_backward(seg_col, seg_row, qkv, totals, grad, rows, which):
    d = qkv.shape[1] // 3
    pairs = d // (2 * HDIM)

    def block(offset):
        return pl.BlockSpec((rows, 2 * HDIM), lambda h: (which, offset + h))

    return call(
        attend_back_kernel,
        (pairs,),
        [
            pl.BlockSpec((rows, 1), lambda h: (which, 0)),
            pl.BlockSpec((1, 1, rows), lambda h: (which, 0, 0)),
            block(0),
            block(pairs),
            block(2 * pairs),
            block(0),
            block(0),
        ],
        [((rows, 3 * d), BF16, whole(rows, 3 * d))],
        (seg_col, seg_row, qkv, qkv, qkv, totals, grad),
        10 * rows * rows * d * 2,
        [pltpu.VMEM((rows, rows), F32)],
    )[0]


def qkv_weight_kernel(micro, rows, where_ref, *refs):
    grads, normed_ref = refs[:micro], refs[micro]
    sum_ref, mine, theirs, parts, part_sems = refs[micro + 1 :]
    total, sums = 0.0, 0.0
    m = normed_ref.shape[0] // micro
    for b, grad_ref in enumerate(grads):
        grad = grad_ref[...]
        sums += column_sum(grad.astype(F32))
        total += tn(grad, normed_ref[b * m : (b + 1) * m])
    sum_ref[...] = sums
    shares(total, 0, rows, where_ref, parts, part_sems, mine, theirs)


def qkv_weight_grad(grads, normed, where):
    m, d = normed.shape
    half, rows = PLACES // 2, 3 * d // PLACES
    step = 8 * rows
    block = pl.BlockSpec((grads[0].shape[0], step), lambda i, *_: (0, i))
    return call(
        functools.partial(qkv_weight_kernel, len(grads), rows),
        (3 * d // step,),
        [block] * len(grads) + [whole(m, d)],
        [
            ((1, 3 * d), F32, pl.BlockSpec((1, step), lambda i, *_: (0, i))),
            ((half, rows, d), BF16, ANY),
            ((half, rows, d), BF16, ANY),
        ],
        (*grads, normed),
        6 * m * d * d,
        [pltpu.VMEM((2, step, d), BF16), pltpu.SemaphoreType.DMA((2, 8))],
        (where,),
    )


def first_norm_kernel(micro, *refs):
    grads = refs[:micro]
    w_ref, x_ref, hidden_ref, vector_ref = refs[micro : micro + 4]
    out_ref, gain_sum_ref, shift_sum_ref, acc_ref = refs[micro + 4 :]
    step = pl.program_id(0)
    rows = grads[0].shape[0]
    for b, grad_ref in enumerate(grads):
        at = pl.ds(b * rows, rows)
        part = nn(grad_ref[...], w_ref[...])

        @pl.when(step == 0)
        def _():
            acc_ref[at] = part

        @pl.when(step > 0)
        def _():
            acc_ref[at] += part

    @pl.when(step == pl.num_programs(0) - 1)
    def _():
        grad = acc_ref[...]
        normal, inverse = centre(x_ref[...].astype(F32))
        gain_sum_ref[...] = column_sum(grad * normal)
        shift_sum_ref[...] = column_sum(grad)
        gain = vector_ref[GAIN_ONE : GAIN_ONE + 1]
        out_ref[...] = hidden_ref[...] + norm_back(grad, normal, inverse, gain)


def first_norm_backward(grads, w, x, grad_hidden, vectors):
    m, d = x.shape
    rows = grads[0].shape[0]
    step = 3 * d // 3
    return call(
        functools.partial(first_norm_kernel, len(grads)),
        (3 * d // step,),
        [cols(rows, step)] * len(grads)
        + [tall(step, d), whole(m, d), whole(m, d), whole(VECTORS, d)],
        [((m, d), F32, whole(m, d))] + [((1, d), F32, whole(1, d))] * 2,
        (*grads, w, x, grad_hidden, vectors),
        6 * m * d * d,
        [pltpu.VMEM((m, d), F32)],
    )


def padded(rows):
    return -(-rows // 16) * 16


def pad_rows(value, rows):
    return jnp.pad(value, ((0, 0),) * (value.ndim - 2) + ((0, rows - value.shape[-2]), (0, 0)))


def body(
    grid,
    tokens,
    segment_ids,
    cotangent,
    norm1_gain,
    norm1_bias,
    qkv_weight,
    qv_bias,
    proj_weight,
    proj_bias,
    norm2_gain,
    norm2_bias,
    fc1_weight,
    fc1_bias,
    fc2_weight,
    fc2_bias,
):
    micro, rows, width = tokens.shape
    n = grid.count
    all_rows = micro * rows
    me = lax.axis_index(AXIS)
    table = lax.dynamic_index_in_dim(jnp.asarray(grid.table()), me, 0, keepdims=False)
    where = lax.dynamic_index_in_dim(jnp.asarray(grid.where()), me, 0, keepdims=False)
    smalls = (
        norm1_gain,
        norm1_bias,
        qv_bias,
        proj_bias,
        norm2_gain,
        norm2_bias,
        fc1_bias,
        fc2_bias,
    )
    sizes = [v.shape[0] for v in smalls]
    r_qkv, r_proj, r_fc1 = (w.shape[1] for w in (qkv_weight, proj_weight, fc1_weight))
    r_fc2 = fc2_weight.shape[1]
    direct = n == PLACES
    splits_one = [padded(r_qkv), 8]
    splits_two = [padded(r_fc1), padded(r_proj)]

    shard_one = first_shard(pad_rows(qkv_weight.T, splits_one[0]), smalls)
    shard_two = jnp.concatenate(
        [pad_rows(fc1_weight.T, splits_two[0]), pad_rows(proj_weight.T, splits_two[1])]
    )
    x = tokens.reshape(all_rows, width)
    cot = cotangent.reshape(all_rows, width)
    seg_col = segment_ids.reshape(all_rows, 1)
    seg_row = segment_ids.reshape(micro, 1, rows)
    valid = (seg_col >= 0).astype(F32)
    grad_mlp = jnp.where(valid > 0, cot, 0)
    line_one, ready = gather_line(
        grid, shard_one, (shard_two, table, where, seg_col, seg_row, valid, grad_mlp)
    )
    shard_two, table, where, seg_col, seg_row, valid, grad_mlp = ready
    line_two = gather_line(grid, shard_two)
    line_three = gather_line(grid, fc2_weight.T)
    parts_one = gather_sides(grid, line_one)
    parts_two = gather_sides(grid, line_two)
    parts_three = gather_sides(grid, line_three)
    if direct:
        places = small_places = table
        qkv_parts = small_parts = parts_one
        fc1_parts = proj_parts = parts_two
        proj_row = r_fc1
    else:
        qkv_all, small_all = put_in_order(parts_one, table, splits_one)
        fc1_all, proj_all = put_in_order(parts_two, table, splits_two)
        (fc2_all,) = put_in_order(parts_three, table, [r_fc2])
        places = jnp.arange(PLACES, dtype=jnp.int32)
        small_places = jnp.arange(n, dtype=jnp.int32)
        where = jnp.concatenate([places // 2, jnp.zeros((1,), jnp.int32)])
        qkv_parts = [qkv_all[:, :r_qkv].reshape(PLACES, -1, width)]
        small_parts = [small_all]
        fc1_parts = [fc1_all[:, :r_fc1].reshape(PLACES, -1, width)]
        proj_parts = [proj_all[:, :r_proj].reshape(PLACES, -1, width)]
        parts_three = [fc2_all.reshape(PLACES, -1, fc2_all.shape[2])]
        proj_row = 0

    normed_one, qkv, vectors, fc1_b, qkv_t = qkv_forward(
        x, qkv_parts, places, small_parts, small_places, sizes
    )
    attended, totals = attend(seg_col, seg_row, qkv, rows)
    hidden, normed_two, activated, slope, mine, theirs, grad_fc2_b, proj_t, fc1_t = mlp_forward(
        attended, x, valid, vectors, fc1_b, grad_mlp, proj_parts, proj_row, fc1_parts, places, where
    )

    def reduce_group(mine, theirs, pieces):
        if not direct:
            ordered = jnp.stack([mine, theirs], axis=1).reshape(PLACES, *mine.shape[1:])
            cut, at = [], 0
            for own, kept in pieces:
                part = ordered[:, at : at + own * n // PLACES]
                cut.append(pad_rows(part.reshape(n, own, -1), kept))
                at += own * n // PLACES
            mine, theirs = pack(cut, table, grid.half)
        return scatter_sum(grid, mine, theirs)

    share_fc2 = reduce_group(mine, theirs, [(r_fc2, r_fc2)])
    (
        grad_fc1_b,
        mine,
        theirs,
        fc2_t,
        grad_hidden,
        grad_branch,
        grad_gain_two,
        grad_shift_two,
        grad_proj_b,
    ) = mlp_backward(
        grad_mlp,
        slope,
        normed_two,
        fc1_t.reshape(-1, width),
        hidden,
        cot,
        valid,
        vectors,
        parts_three,
        places,
        where,
        width // PLACES,
    )
    grad_att, mine, theirs = proj_backward(
        grad_branch, attended, proj_t.reshape(width, width), where, mine, theirs
    )
    share_two = reduce_group(mine, theirs, [(r_fc1, splits_two[0]), (r_proj, splits_two[1])])
    grad_qkv = [
        attend_backward(seg_col, seg_row, qkv, totals, grad_att, rows, b)
        for b in range(micro)
    ]
    sums, mine, theirs = qkv_weight_grad(grad_qkv, normed_one, where)
    share_one = reduce_group(mine, theirs, [(r_qkv, splits_one[0])])
    input_grad, grad_gain_one, grad_shift_one = first_norm_backward(
        grad_qkv, qkv_t.reshape(-1, width), x, grad_hidden, vectors
    )
    output = fc2_forward(
        activated, fc2_t.reshape(width, -1), vectors, hidden, valid
    )

    small_grads = jnp.concatenate(
        [
            grad_gain_one,
            grad_shift_one,
            sums[:, :width],
            sums[:, 2 * width :],
            grad_proj_b,
            grad_gain_two,
            grad_shift_two,
            grad_fc1_b.reshape(-1, width),
            grad_fc2_b,
            jnp.zeros((VECTORS - FC2 - 1, width), F32),
        ]
    )
    small_grads = sum_everywhere(grid, small_grads)
    own, row = [], 0
    for size in sizes:
        at = me * size
        place = (row + at // width, at % width)
        own.append(lax.dynamic_slice(small_grads, place, (1, size)).reshape(size))
        row += -(-size * n // width)
    s_gain_one, s_shift_one, s_qv, s_proj, s_gain_two, s_shift_two, s_fc1, s_fc2 = own
    return (
        output.reshape(micro, rows, width),
        input_grad.reshape(micro, rows, width),
        s_gain_one,
        s_shift_one,
        share_one[:r_qkv].T,
        s_qv,
        share_two[splits_two[0] : splits_two[0] + r_proj].T,
        s_proj,
        s_gain_two,
        s_shift_two,
        share_two[:r_fc1].T,
        s_fc1,
        share_fc2.T,
        s_fc2,
    )


def solution(mesh):
    row = P(None, AXIS, None)
    vec = P(AXIS)
    mat = P(None, AXIS)
    grid = Grid(mesh.size)

    def layer(*args):
        return body(grid, *args)

    return jax.shard_map(
        layer,
        mesh=mesh,
        in_specs=(row, mat, row) + (vec, vec, mat, vec, mat, vec) * 2,
        out_specs=(row, row) + (vec, vec, mat, vec, mat, vec) * 2,
        check_vma=False,
    )
```
